256 devices in a mesh: section: 16 (over z, x_hi), fsdp: 16 (over x_lo, y, core).
Axes of the slice: x: 4 (x_hi: 2, x_lo: 2; x = x_hi * 2 + x_lo), y: 4, z: 8, core: 2. Of those that a mesh axis runs over, the one named last changes fastest.
Arguments:
- x_fwd: bfloat16 [16, 384, 4096], P('section', None, 'fsdp'), may hold values from -6 to 6
- x_saved: bfloat16 [16, 384, 4096], P('section', None, 'fsdp'), may hold values from -6 to 6
- cotangent: bfloat16 [16, 384, 4096], P('section', None, 'fsdp'), may hold values from -6 to 6
- qkv_weight: bfloat16 [16, 4096, 3, 4096], P('section', None, None, 'fsdp')
- gain: float32 [16, 4096], P('section', 'fsdp'), may hold values from 0.1 to 1.9
- block_lists: int32 [8, 3, 2], replicated, may hold values from 0 to 2, as said below
- plan: int32 [16, 2], P('section'), may hold values from 0 to 7
Outputs:
- y_next: bfloat16 [16, 384, 4096], P('section', None, 'fsdp')
- dx_prev: bfloat16 [16, 384, 4096], P('section', None, 'fsdp')
- w_grad: bfloat16 [16, 4096, 3, 4096], P('section', None, None, 'fsdp')
- gain_grad: float32 [16, 4096], P('section', 'fsdp')
The draws below stay inside these ranges and needn't reach their ends.
Inputs may be any that keep to these rules, and one draw needn't show every extreme that they name: block_lists[z, b, 0] = b; the 2 entries of a row are distinct.
All inputs are finite; a program needn't handle non-finite values.
Results may differ from the reference program's by a relative error of at most 0.024.
Values may be sent and summed in bfloat16 or wider, within the bound.
No kernel may reach another device: no remote copies, remote signals or barrier semaphores. Data moves between devices by JAX's collectives and lax.ppermute only.
A program may use at most 128 MiB of HBM per device.

```python
import math
import jax
import jax.numpy as jnp
from jax import lax

D = 4096
HD = 128
BLK = 128
BAND = 2
SLICES = 8
TOK = 384
SECTIONS = 16
QBLOCKS = 3


def draw_qkv_weight(key, part):
    key_list = jax.random.split(key, 1)
    noise_all = jax.random.normal(key_list[0], (SECTIONS, D, 3, D), jnp.float32)
    scales = jnp.array([1.6, 1.6, 1.0], jnp.float32).reshape(1, 1, 3, 1)
    return (noise_all * scales * (1.0 / math.sqrt(D))).astype(jnp.bfloat16)


def draw_block_lists(key, part):
    column_ids = jnp.arange(QBLOCKS, dtype=jnp.int32)
    scores = jax.random.randint(key, (SLICES, QBLOCKS, QBLOCKS), 0, 4096) * QBLOCKS + column_ids[None, None, :]
    own_mask = column_ids[:, None] == column_ids[None, :]
    scores = jnp.where(own_mask[None, :, :], -1, scores)
    ranked = jnp.argsort(scores, axis=2, stable=True)
    return ranked[:, :, :BAND].astype(jnp.int32)


def draw_plan(key, part):
    key_list = jax.random.split(key, 2)
    offset = jax.random.randint(key_list[0], (), 0, SLICES)
    values = (jnp.arange(2 * SECTIONS, dtype=jnp.int32) + offset) % SLICES
    return jax.random.permutation(key_list[1], values).reshape(SECTIONS, 2).astype(jnp.int32)


def shard_levels(stream_key, shape, shards, smallest, high):
    level = 1.0
    for position, parts in shards:
        draws = jax.random.uniform(jax.random.fold_in(jax.random.fold_in(stream_key, 6), position), (parts,), jnp.float32, smallest / len(shards), high / len(shards))
        level = level * jnp.repeat(jnp.exp(draws), shape[position] // parts).reshape((-1,) + (1,) * (len(shape) - 1 - position))
    return level


def gaussian(stream_key, shape, scale, most, shards=(), held_as=jnp.bfloat16):
    values = jax.random.normal(stream_key, shape, jnp.float32) * scale
    if len(shards) > 0:
        values = shard_levels(stream_key, shape, shards, -0.22, 0.18) * values
    return jnp.clip(values, min=-most, max=most).astype(held_as)


def setup_inputs(seed: int = 0) -> dict:
    splits = jax.random.split(jax.random.key(seed), 8)
    return {
        "x_fwd": gaussian(splits[0], (SECTIONS, TOK, D), 1.0, 6.0, ((0, 16), (2, 16))),
        "x_saved": gaussian(splits[1], (SECTIONS, TOK, D), 1.0, 6.0, ((0, 16), (2, 16))),
        "cotangent": gaussian(splits[2], (SECTIONS, TOK, D), 1.0, 6.0, ((0, 16), (2, 16))),
        "qkv_weight": draw_qkv_weight(jax.random.fold_in(splits[7], 71), 0),
        "gain": jnp.clip(1.0 + 0.18 * jax.random.normal(splits[4], (SECTIONS, D), jnp.float32), 0.1, 1.9),
        "block_lists": draw_block_lists(jax.random.fold_in(splits[7], 71), 0),
        "plan": draw_plan(jax.random.fold_in(splits[7], 71), 0),
    }


EPS = 1e-05

def attend(query, key_in, value, block_ids):
    tokens, feat_width = query.shape
    head_count = feat_width // HD
    block_count = tokens // BLK
    band_size = block_ids.shape[1]
    q_blocks = query.reshape(block_count, BLK, head_count, HD)
    k_rows = key_in.reshape(block_count, BLK, head_count, HD)[block_ids].reshape(block_count, band_size * BLK, head_count, HD)
    v_rows = value.reshape(block_count, BLK, head_count, HD)[block_ids].reshape(block_count, band_size * BLK, head_count, HD)
    scores = jnp.einsum('qthd,qshd->qhts', q_blocks.astype(jnp.float32), k_rows.astype(jnp.float32)) * (1.0 / math.sqrt(HD))
    row_max = lax.optimization_barrier(jnp.max(scores, axis=3, keepdims=True))
    expd = jnp.exp(scores - row_max)
    probs = expd / lax.optimization_barrier(jnp.sum(expd, axis=3, keepdims=True))
    probs_low = probs.astype(jnp.bfloat16)
    output = jnp.einsum('qhts,qshd->qthd', probs_low.astype(jnp.float32), v_rows.astype(jnp.float32)).reshape(tokens, feat_width)
    return (output, (probs, probs_low, q_blocks, k_rows, v_rows))

def attend_back(upstream, block_ids, saved):
    probs, probs_low, q_blocks, k_rows, v_rows = saved
    block_count, block_len, head_count, head_size = q_blocks.shape
    band_size = block_ids.shape[1]
    tokens = block_count * block_len
    c_blocks = upstream.reshape(block_count, block_len, head_count, head_size).astype(jnp.float32)
    grad_vrows = jnp.einsum('qhts,qthd->qshd', probs_low.astype(jnp.float32), c_blocks)
    grad_p = jnp.einsum('qthd,qshd->qhts', c_blocks, v_rows.astype(jnp.float32))
    grad_s = probs * (grad_p - lax.optimization_barrier(jnp.sum(probs * grad_p, axis=3, keepdims=True))) * (1.0 / math.sqrt(HD))
    grad_s_low = grad_s.astype(jnp.bfloat16)
    grad_q = jnp.einsum('qhts,qshd->qthd', grad_s_low.astype(jnp.float32), k_rows.astype(jnp.float32))
    grad_krows = jnp.einsum('qhts,qthd->qshd', grad_s_low.astype(jnp.float32), q_blocks.astype(jnp.float32))
    onehot = (block_ids[:, :, None] == jnp.arange(block_count, dtype=jnp.int32)[None, None, :]).astype(jnp.float32)
    band_shape = (block_count, band_size, block_len, head_count, head_size)
    grad_k = jnp.einsum('qbk,qbthd->kthd', onehot, grad_krows.reshape(band_shape))
    grad_v = jnp.einsum('qbk,qbthd->kthd', onehot, grad_vrows.reshape(band_shape))
    return (grad_q.reshape(tokens, -1), grad_k.reshape(tokens, -1), grad_v.reshape(tokens, -1))

def project(x_in, gain_row, w_flat):
    x_wide = x_in.astype(jnp.float32)
    row_scale = lax.rsqrt(lax.optimization_barrier(jnp.mean(x_wide * x_wide, axis=1)) + EPS)
    scaled_in = (x_wide * gain_row[None, :]).astype(jnp.bfloat16)
    product = jnp.dot(scaled_in, w_flat, preferred_element_type=jnp.float32)
    projected = (row_scale[:, None] * product).astype(jnp.bfloat16)
    return (x_wide, row_scale, scaled_in, projected)

def reference(x_fwd, x_saved, cotangent, qkv_weight, gain, block_lists, plan):

    def section_step(section_args):
        forward_in, saved_in, upstream, weight, gain_row, sched_row = section_args
        w_flat = weight.reshape(D, 3 * D)
        tokens = forward_in.shape[0]
        wide_fwd, scale_fwd, scaled_fwd, proj_fwd = project(forward_in, gain_row, w_flat)
        lists_fwd = block_lists[sched_row[0]]
        attn_fwd = attend(proj_fwd[:, :D], proj_fwd[:, D:2 * D], proj_fwd[:, 2 * D:], lists_fwd)[0]
        result = (wide_fwd + attn_fwd).astype(jnp.bfloat16)
        wide_bwd, scale_bwd, scaled_bwd, proj_bwd = project(saved_in, gain_row, w_flat)
        lists_bwd = block_lists[sched_row[1]]
        saved = attend(proj_bwd[:, :D], proj_bwd[:, D:2 * D], proj_bwd[:, 2 * D:], lists_bwd)[1]
        grad_q, grad_k, grad_v = attend_back(upstream, lists_bwd, saved)
        stacked = jnp.stack([grad_q, grad_k, grad_v], axis=1).reshape(tokens, 3 * D)
        grads = (scale_bwd[:, None] * stacked).astype(jnp.bfloat16)
        grad_w = lax.dot_general(scaled_bwd, grads, (((0,), (0,)), ((), ())), preferred_element_type=jnp.float32)
        grad_w = grad_w.astype(jnp.bfloat16).reshape(D, 3, D)
        grad_in = lax.dot_general(grads, w_flat, (((1,), (1,)), ((), ())), preferred_element_type=jnp.float32)
        row_total = lax.optimization_barrier(jnp.sum(scaled_bwd.astype(jnp.float32) * grad_in, axis=1))
        grad_x = upstream.astype(jnp.float32) + gain_row[None, :] * grad_in
        grad_x = grad_x - (scale_bwd * scale_bwd * row_total / D)[:, None] * wide_bwd
        grad_gain = lax.optimization_barrier(jnp.sum(wide_bwd * grad_in, axis=0))
        return (result, grad_x.astype(jnp.bfloat16), grad_w, grad_gain)
    results, grad_xs, grad_ws, grad_gains = lax.map(section_step, (x_fwd, x_saved, cotangent, qkv_weight, gain, plan))
    return (jnp.roll(results, 1, axis=0), jnp.roll(grad_xs, -1, axis=0), grad_ws, grad_gains)
```

```python
import math

import jax
import jax.numpy as jnp
from jax import lax
from jax.experimental import pallas as pl
from jax.experimental.pallas import tpu as pltpu
from jax.sharding import PartitionSpec as P

HD = 128
BLK = 128
EPS = 1e-05
STAT = 16
CHIPS = 8
F32 = jnp.float32
BF16 = jnp.bfloat16
VMEM_BYTES = 40 << 20


def pieces(row):
    high = row.astype(BF16).astype(F32)
    rest = row - high
    mid = rest.astype(BF16).astype(F32)
    return high, mid, rest - mid


def stat_rows(row, width):
    span = row.shape[1]
    index = lax.broadcasted_iota(jnp.int32, (STAT, width), 0)
    out = jnp.zeros((STAT, width), F32)
    for i, part in enumerate(pieces(row)):
        for j, start in enumerate(range(0, span, width)):
            held = part[:, start : start + width]
            if held.shape[1] < width:
                held = jnp.concatenate(
                    [held, jnp.zeros((1, width - held.shape[1]), F32)], axis=1
                )
            out = jnp.where(index == 3 * j + i, jnp.broadcast_to(held, (STAT, width)), out)
    return out.astype(BF16)


def stat_row(rows, span):
    width = rows.shape[1]
    parts = []
    for j, start in enumerate(range(0, span, width)):
        part = rows[3 * j : 3 * j + 1] + rows[3 * j + 1 : 3 * j + 2] + rows[3 * j + 2 : 3 * j + 3]
        parts.append(part[:, : min(width, span - start)])
    return parts[0] if len(parts) == 1 else jnp.concatenate(parts, axis=1)


def as_column(row):
    return jnp.transpose(jnp.broadcast_to(row, (HD, row.shape[1])))


def row_sums(folded):
    return jnp.sum(jnp.transpose(folded), axis=0, keepdims=True)


def pack_kernel(x_ref, gain_ref, out_ref):
    tokens = x_ref.shape[0]
    wide = x_ref[...].astype(F32)
    out_ref[:tokens, :] = (wide * gain_ref[...]).astype(BF16)
    squares = wide * wide
    folded = squares[:, :HD]
    for start in range(HD, squares.shape[1], HD):
        folded = folded + squares[:, start : start + HD]
    out_ref[tokens:, :] = stat_rows(row_sums(folded), out_ref.shape[1])


def block_mask(ints_ref, which, b, tokens):
    z = ints_ref[48 + which]
    column = lax.shift_right_logical(
        lax.broadcasted_iota(jnp.int32, (BLK, tokens), 1), BLK.bit_length() - 1
    )
    first = ints_ref[z * 6 + b * 2]
    second = ints_ref[z * 6 + b * 2 + 1]
    return (column == first) | (column == second)


def probabilities(query, key_in, mask):
    scores = lax.dot_general(
        query, key_in, (((1,), (1,)), ((), ())), preferred_element_type=F32
    ) * (1.0 / math.sqrt(HD))
    scores = jnp.where(mask, scores, -1e30)
    expd = jnp.exp(scores - jnp.max(scores, axis=1, keepdims=True))
    return expd / jnp.sum(expd, axis=1, keepdims=True)


def accumulate(mine_ref, other_ref, w_refs, acc_ref, stat_ref, tokens):
    step = pl.program_id(0)
    pairs = mine_ref.shape[0]
    local = mine_ref.shape[2]
    x_all = jnp.concatenate(
        [ref[i, :tokens, :] for i in range(pairs) for ref in (mine_ref, other_ref)], axis=1
    )
    stats = sum(
        ref[i, tokens:, :].astype(F32) for i in range(pairs) for ref in (mine_ref, other_ref)
    )
    for j in range(3):
        w_all = jnp.concatenate([ref[j] for ref in w_refs], axis=0)
        part = jnp.dot(x_all, w_all, preferred_element_type=F32)
        cols = slice(j * local, (j + 1) * local)

        @pl.when(step == 0)
        def _():
            acc_ref[:, cols] = part

        @pl.when(step > 0)
        def _():
            acc_ref[:, cols] += part

    @pl.when(step == 0)
    def _():
        stat_ref[...] = stats

    @pl.when(step > 0)
    def _():
        stat_ref[...] += stats


def row_scale(stat_ref, tokens, width):
    return lax.rsqrt(as_column(stat_row(stat_ref[...], tokens)) / width + EPS)


def project(acc_ref, scale, proj_ref):
    for start in range(0, acc_ref.shape[1], HD):
        proj_ref[:, start : start + HD] = (scale * acc_ref[:, start : start + HD]).astype(BF16)


def forward_kernel(ints_ref, mine_ref, other_ref, *refs):
    w_refs, (x_ref, out_ref, acc_ref, stat_ref, proj_ref) = refs[:-5], refs[-5:]
    tokens, local = x_ref.shape
    accumulate(mine_ref, other_ref, w_refs, acc_ref, stat_ref, tokens)

    @pl.when(pl.program_id(0) == pl.num_programs(0) - 1)
    def _():
        scale = row_scale(stat_ref, tokens, 2 * CHIPS * local)
        project(acc_ref, scale, proj_ref)
        for h in range(local // HD):
            at = h * HD
            key_in = proj_ref[:, local + at : local + at + HD]
            value = proj_ref[:, 2 * local + at : 2 * local + at + HD]
            for b in range(tokens // BLK):
                rows = slice(b * BLK, (b + 1) * BLK)
                probs = probabilities(
                    proj_ref[rows, at : at + HD], key_in, block_mask(ints_ref, 0, b, tokens)
                )
                attn = jnp.dot(probs.astype(BF16), value, preferred_element_type=F32)
                out_ref[rows, at : at + HD] = (
                    x_ref[rows, at : at + HD].astype(F32) + attn
                ).astype(BF16)


def backward_kernel(ints_ref, mine_ref, other_ref, *refs):
    w_refs = refs[:-8]
    c_ref, out_ref, scale_ref, acc_ref, stat_ref, proj_ref, p_ref, s_ref = refs[-8:]
    tokens, local = c_ref.shape
    accumulate(mine_ref, other_ref, w_refs, acc_ref, stat_ref, tokens)

    @pl.when(pl.program_id(0) == pl.num_programs(0) - 1)
    def _():
        scale = row_scale(stat_ref, tokens, 2 * CHIPS * local)
        scale_ref[...] = scale
        project(acc_ref, scale, proj_ref)
        over_tokens = (((0,), (0,)), ((), ()))
        folded = jnp.zeros((tokens, HD), F32)
        for h in range(local // HD):
            at = h * HD
            query = proj_ref[:, at : at + HD]
            key_in = proj_ref[:, local + at : local + at + HD]
            value = proj_ref[:, 2 * local + at : 2 * local + at + HD]
            upstream = c_ref[:, at : at + HD]
            for b in range(tokens // BLK):
                rows = slice(b * BLK, (b + 1) * BLK)
                probs = probabilities(query[rows], key_in, block_mask(ints_ref, 1, b, tokens))
                grad_p = lax.dot_general(
                    upstream[rows], value, (((1,), (1,)), ((), ())), preferred_element_type=F32
                )
                inner = jnp.sum(probs * grad_p, axis=1, keepdims=True)
                p_ref[rows, :] = probs.astype(BF16)
                s_ref[rows, :] = (probs * (grad_p - inner) * (1.0 / math.sqrt(HD))).astype(BF16)
            grad_s = s_ref[...]
            parts = (
                jnp.dot(grad_s, key_in, preferred_element_type=F32),
                lax.dot_general(grad_s, query, over_tokens, preferred_element_type=F32),
                lax.dot_general(p_ref[...], upstream, over_tokens, preferred_element_type=F32),
            )
            for j, part in enumerate(parts):
                cols = slice(j * local + at, j * local + at + HD)
                grads = (scale * part).astype(BF16)
                out_ref[:tokens, cols] = grads
                folded = folded + grads.astype(F32) * acc_ref[:, cols]
        out_ref[tokens:, :] = stat_rows(row_sums(folded), out_ref.shape[1])


def weight_specs(pairs, local, part):
    def spec(i, side):
        return pl.BlockSpec((3, local, local), lambda d, ints: (0, ints[part + side * 8 + d * pairs + i], 0))

    return [spec(i, side) for i in range(pairs) for side in range(2)]


def attention_call(kernel, ints, mine, other, weight, extra, out_shapes, scratch, pairs, name):
    chips, rows, local = mine.shape
    whole = lambda shape: pl.BlockSpec(shape, lambda d, ints: (0,) * len(shape))
    blocks = pl.BlockSpec((pairs, rows, local), lambda d, ints: (d, 0, 0))
    tokens = extra.shape[0]
    specs = weight_specs(pairs, local, 50)
    return pl.pallas_call(
        kernel,
        out_shape=out_shapes,
        grid_spec=pltpu.PrefetchScalarGridSpec(
            num_scalar_prefetch=1,
            grid=(chips // pairs,),
            in_specs=[blocks, blocks, *specs, whole(extra.shape)],
            out_specs=jax.tree.map(lambda s: whole(s.shape), out_shapes),
            scratch_shapes=[
                pltpu.VMEM((tokens, 3 * local), F32),
                pltpu.VMEM((STAT, local), F32),
                pltpu.VMEM((tokens, 3 * local), BF16),
                *scratch,
            ],
        ),
        compiler_params=pltpu.CompilerParams(vmem_limit_bytes=VMEM_BYTES),
        name=name,
    )(ints, mine, other, *([weight] * len(specs)), extra)


def input_grad_kernel(ints_ref, mine_ref, other_ref, w_mine_ref, w_other_ref, *out_refs):
    tokens = mine_ref.shape[0] - STAT
    local = out_refs[0].shape[1]
    step = pl.program_id(0)
    grads = jnp.concatenate([mine_ref[:tokens, :], other_ref[:tokens, :]], axis=1)
    w_all = jnp.concatenate([ref[j] for ref in (w_mine_ref, w_other_ref) for j in range(3)], axis=1)
    part = lax.dot_general(
        grads, w_all, (((1,), (1,)), ((), ())), preferred_element_type=F32
    ).astype(BF16)
    totals = stat_row(mine_ref[tokens:, :].astype(F32) + other_ref[tokens:, :].astype(F32), tokens)
    stats = stat_rows(totals, local)
    for i, ref in enumerate(out_refs):

        @pl.when(step == i)
        def _():
            ref[:tokens, :] = part
            ref[tokens:, :] = stats


def input_grad(ints, mine, other, weight, w_other, first, count, name):
    rows = mine.shape[0]
    local = weight.shape[2]
    whole = lambda shape: pl.BlockSpec(shape, lambda d, ints: (0,) * len(shape))
    w_spec = pl.BlockSpec((3, local, local), lambda d, ints: (0, ints[50 + first + d], 0))
    return pl.pallas_call(
        input_grad_kernel,
        out_shape=[jax.ShapeDtypeStruct((rows, local), BF16)] * count,
        grid_spec=pltpu.PrefetchScalarGridSpec(
            num_scalar_prefetch=1,
            grid=(count,),
            in_specs=[whole(mine.shape), whole(other.shape), w_spec, w_spec],
            out_specs=[whole((rows, local))] * count,
        ),
        compiler_params=pltpu.CompilerParams(vmem_limit_bytes=VMEM_BYTES),
        name=name,
    )(ints, mine, other, weight, w_other)


def weight_grad_kernel(ints_ref, mine_ref, other_ref, g_ref, out_ref):
    tokens = g_ref.shape[0] - STAT
    local = mine_ref.shape[2]
    side = ints_ref[66]
    grads = g_ref[:tokens, :]
    for ref, at in ((mine_ref, side), (other_ref, 1 - side)):
        part = lax.dot_general(
            ref[0, :tokens, :], grads, (((0,), (0,)), ((), ())), preferred_element_type=F32
        )
        for j in range(3):
            out_ref[j, pl.ds(pl.multiple_of(at * local, local), local), :] = part[
                :, j * local : (j + 1) * local
            ].astype(BF16)


def weight_grad(ints, mine, other, grads):
    chips, rows, local = mine.shape
    blocks = pl.BlockSpec((1, rows, local), lambda d, ints: (d, 0, 0))
    return pl.pallas_call(
        weight_grad_kernel,
        out_shape=jax.ShapeDtypeStruct((3, 2 * chips * local, local), BF16),
        grid_spec=pltpu.PrefetchScalarGridSpec(
            num_scalar_prefetch=1,
            grid=(chips,),
            in_specs=[blocks, blocks, pl.BlockSpec(grads.shape, lambda d, ints: (0, 0))],
            out_specs=pl.BlockSpec((3, 2 * local, local), lambda d, ints: (0, ints[67 + d], 0)),
        ),
        compiler_params=pltpu.CompilerParams(vmem_limit_bytes=VMEM_BYTES),
        name="weight_grad",
    )(ints, mine, other, grads)


def finish_kernel(*refs):
    blocks, (x_ref, c_ref, gain_ref, scale_ref, dx_ref, gg_ref) = refs[:CHIPS], refs[CHIPS:]
    tokens, local = x_ref.shape
    own_in = blocks[0][:tokens, :].astype(F32)
    stats = blocks[0][tokens:, :].astype(F32)
    for ref in blocks[1:]:
        own_in = own_in + ref[:tokens, :].astype(F32)
        stats = stats + ref[tokens:, :].astype(F32)
    total = as_column(stat_row(stats, tokens))
    scale = scale_ref[...]
    factor = scale * scale * total / (2 * CHIPS * local)
    x_wide = x_ref[...].astype(F32)
    for start in range(0, local, HD):
        cols = slice(start, start + HD)
        grad_x = c_ref[:, cols].astype(F32) + gain_ref[:, cols] * own_in[:, cols]
        dx_ref[:, cols] = (grad_x - factor * x_wide[:, cols]).astype(BF16)
    gg_ref[...] = jnp.sum(x_wide * own_in, axis=0, keepdims=True)


def plain_call(kernel, out_shape, name, *args):
    return pl.pallas_call(
        kernel,
        out_shape=out_shape,
        compiler_params=pltpu.CompilerParams(vmem_limit_bytes=VMEM_BYTES),
        name=name,
    )(*args)


def to_chip(block, distance):
    route = [(i, ((i >> 1) ^ distance) << 1 | (i & 1)) for i in range(2 * CHIPS)]
    return lax.ppermute(block, "fsdp", route)


def to_core(block):
    return lax.ppermute(block, "fsdp", [(i, i ^ 1) for i in range(2 * CHIPS)])


def shifted(block, axis, distance):
    count = lax.axis_size(axis)
    return lax.ppermute(block, axis, [((i - distance) % count, i) for i in range(count)])


def gathered(block):
    return jnp.stack([block] + [to_chip(block, d) for d in range(1, CHIPS)])


def on_device(x_fwd, x_saved, cotangent, qkv_weight, gain, block_lists, plan):
    forward_in = x_fwd[0]
    saved_in = x_saved[0]
    upstream = cotangent[0]
    weight = jnp.transpose(qkv_weight[0], (1, 0, 2))
    tokens, local = forward_in.shape
    me = lax.axis_index("fsdp").astype(jnp.int32)
    chip, side = me // 2, me % 2
    apart = jnp.arange(CHIPS, dtype=jnp.int32) ^ chip
    ints = jnp.concatenate(
        [
            block_lists.reshape(-1),
            plan.reshape(-1),
            apart * 2 + side,
            apart * 2 + 1 - side,
            side[None],
            apart,
        ]
    )
    packed = jax.ShapeDtypeStruct((tokens + STAT, local), BF16)
    pay_bwd = plain_call(pack_kernel, packed, "pack_bwd", saved_in, gain)
    pay_fwd = plain_call(pack_kernel, packed, "pack_fwd", forward_in, gain)
    w_other = to_core(weight)

    mine_bwd = gathered(pay_bwd)
    mine_bwd, pay_fwd, w_other = lax.optimization_barrier((mine_bwd, pay_fwd, w_other))
    other_bwd = to_core(mine_bwd)
    grads, scale = attention_call(
        backward_kernel,
        ints,
        mine_bwd,
        other_bwd,
        weight,
        upstream,
        (
            jax.ShapeDtypeStruct((tokens + STAT, 3 * local), BF16),
            jax.ShapeDtypeStruct((tokens, HD), F32),
        ),
        [pltpu.VMEM((tokens, tokens), BF16), pltpu.VMEM((tokens, tokens), BF16)],
        2,
        "backward",
    )
    grads_other = to_core(grads)
    blocks = input_grad(ints, grads, grads_other, weight, w_other, 0, CHIPS, "input_grad")
    blocks = [blocks[0]] + [to_chip(blocks[d], d) for d in range(1, CHIPS)]

    mine_fwd = gathered(pay_fwd)
    other_fwd = to_core(mine_fwd)
    result = attention_call(
        forward_kernel,
        ints,
        mine_fwd,
        other_fwd,
        weight,
        forward_in,
        jax.ShapeDtypeStruct((tokens, local), BF16),
        [],
        2,
        "forward",
    )
    sent_on = shifted(result, "section", 1)
    grad_w = weight_grad(ints, mine_bwd, other_bwd, grads)
    grad_x, grad_gain = plain_call(
        finish_kernel,
        (
            jax.ShapeDtypeStruct((tokens, local), BF16),
            jax.ShapeDtypeStruct((1, local), F32),
        ),
        "finish",
        *blocks,
        saved_in,
        upstream,
        gain,
        scale,
    )
    sent_back = shifted(grad_x, "section", -1)
    return (sent_on[None], sent_back[None], jnp.transpose(grad_w, (1, 0, 2))[None], grad_gain)


def solution(mesh):
    in_specs = (
        P("section", None, "fsdp"),
        P("section", None, "fsdp"),
        P("section", None, "fsdp"),
        P("section", None, None, "fsdp"),
        P("section", "fsdp"),
        P(),
        P("section", None),
    )
    out_specs = (
        P("section", None, "fsdp"),
        P("section", None, "fsdp"),
        P("section", None, None, "fsdp"),
        P("section", "fsdp"),
    )
    return jax.shard_map(
        on_device, mesh=mesh, in_specs=in_specs, out_specs=out_specs, check_vma=False
    )
```

```python
import functools
import math

import jax
import jax.numpy as jnp
from jax import lax
from jax.experimental import pallas as pl
from jax.experimental.pallas import tpu as pltpu
from jax.sharding import PartitionSpec as P

HD = 128
BLK = 128
EPS = 1e-05
STAT = 16
CHIPS = 8
F32 = jnp.float32
BF16 = jnp.bfloat16
VMEM_BYTES = 40 << 20


def pieces(row):
    high = row.astype(BF16).astype(F32)
    rest = row - high
    mid = rest.astype(BF16).astype(F32)
    return high, mid, rest - mid


def stat_rows(row, width):
    span = row.shape[1]
    index = lax.broadcasted_iota(jnp.int32, (STAT, width), 0)
    out = jnp.zeros((STAT, width), F32)
    for i, part in enumerate(pieces(row)):
        for j, start in enumerate(range(0, span, width)):
            held = part[:, start : start + width]
            if held.shape[1] < width:
                held = jnp.concatenate(
                    [held, jnp.zeros((1, width - held.shape[1]), F32)], axis=1
                )
            out = jnp.where(index == 3 * j + i, jnp.broadcast_to(held, (STAT, width)), out)
    return out.astype(BF16)


def stat_row(rows, span):
    width = rows.shape[1]
    parts = []
    for j, start in enumerate(range(0, span, width)):
        part = rows[3 * j : 3 * j + 1] + rows[3 * j + 1 : 3 * j + 2] + rows[3 * j + 2 : 3 * j + 3]
        parts.append(part[:, : min(width, span - start)])
    return parts[0] if len(parts) == 1 else jnp.concatenate(parts, axis=1)


def as_column(row):
    return jnp.transpose(jnp.broadcast_to(row, (HD, row.shape[1])))


def row_sums(folded):
    return jnp.sum(jnp.transpose(folded), axis=0, keepdims=True)


def pack_kernel(x_ref, gain_ref, out_ref):
    tokens = x_ref.shape[0]
    wide = x_ref[...].astype(F32)
    out_ref[:tokens, :] = (wide * gain_ref[...]).astype(BF16)
    squares = wide * wide
    folded = squares[:, :HD]
    for start in range(HD, squares.shape[1], HD):
        folded = folded + squares[:, start : start + HD]
    out_ref[tokens:, :] = stat_rows(row_sums(folded), out_ref.shape[1])


def listed(ints_ref, which, b, shape, dim):
    z = ints_ref[48 + which]
    block = lax.shift_right_logical(
        lax.broadcasted_iota(jnp.int32, shape, dim), BLK.bit_length() - 1
    )
    return (block == ints_ref[z * 6 + b * 2]) | (block == ints_ref[z * 6 + b * 2 + 1])


def contract(left, right, left_dim, right_dim):
    return lax.dot_general(
        left, right, (((left_dim,), (right_dim,)), ((), ())), preferred_element_type=F32
    )


def softmax(scores, mask, axis):
    scores = jnp.where(mask, scores * (1.0 / math.sqrt(HD)), -1e30)
    expd = jnp.exp(scores - jnp.max(scores, axis=axis, keepdims=True))
    return expd * (1.0 / jnp.sum(expd, axis=axis, keepdims=True))


def partial_product(ints_ref, at, mine_ref, other_ref, w_ref, tokens):
    count, _, local = mine_ref.shape
    both = [(ref, i) for i in range(count) for ref in (mine_ref, other_ref)]
    x_all = jnp.concatenate([ref[i, :tokens, :] for ref, i in both], axis=1)
    places = [ints_ref[50 + side * 8 + at + i] for i in range(count) for side in range(2)]
    parts = []
    for j in range(3):
        w_all = jnp.concatenate(
            [w_ref[j, pl.ds(pl.multiple_of(p * local, local), local), :] for p in places], axis=0
        )
        parts.append(jnp.dot(x_all, w_all, preferred_element_type=F32))
    stats = sum(ref[i, tokens:, :].astype(F32) for ref, i in both)
    return parts, stats


def first_kernel(ints_ref, mine_ref, other_ref, w_ref, acc_ref, stat_ref):
    tokens = acc_ref.shape[0]
    local = mine_ref.shape[2]
    parts, stats = partial_product(ints_ref, 0, mine_ref, other_ref, w_ref, tokens)
    for j, part in enumerate(parts):
        acc_ref[:, j * local : (j + 1) * local] = part
    stat_ref[...] = stats


def finish_product(ints_ref, first_ref, stat_ref, mine_ref, other_ref, w_ref, acc_ref, proj_ref):
    tokens = first_ref.shape[0]
    local = mine_ref.shape[2]
    parts, stats = partial_product(ints_ref, 4, mine_ref, other_ref, w_ref, tokens)
    width = 2 * CHIPS * local
    scale = lax.rsqrt(as_column(stat_row(stat_ref[...] + stats, tokens)) / width + EPS)
    for j, part in enumerate(parts):
        for start in range(0, local, HD):
            cols = slice(j * local + start, j * local + start + HD)
            whole = first_ref[:, cols] + part[:, start : start + HD]
            if acc_ref is not None:
                acc_ref[:, cols] = whole
            proj_ref[:, cols] = (scale * whole).astype(BF16)
    return scale


def forward_kernel(
    ints_ref, first_ref, stat_ref, mine_ref, other_ref, w_ref, x_ref, out_ref, proj_ref
):
    tokens, local = x_ref.shape
    finish_product(ints_ref, first_ref, stat_ref, mine_ref, other_ref, w_ref, None, proj_ref)
    for b in range(tokens // BLK):
        rows = slice(b * BLK, (b + 1) * BLK)
        mask = listed(ints_ref, 0, b, (BLK, tokens), 1)
        for h in range(local // HD):
            at = h * HD
            key_in = proj_ref[:, local + at : local + at + HD]
            value = proj_ref[:, 2 * local + at : 2 * local + at + HD]
            scores = contract(proj_ref[rows, at : at + HD], key_in, 1, 1)
            probs = softmax(scores, mask, 1)
            attn = jnp.dot(probs.astype(BF16), value, preferred_element_type=F32)
            out_ref[rows, at : at + HD] = (x_ref[rows, at : at + HD].astype(F32) + attn).astype(
                BF16
            )


def backward_kernel(
    ints_ref,
    first_ref,
    stat_ref,
    mine_ref,
    other_ref,
    w_ref,
    c_ref,
    out_ref,
    scale_ref,
    acc_ref,
    proj_ref,
    p_ref,
    s_ref,
):
    tokens, local = c_ref.shape
    scale = finish_product(
        ints_ref, first_ref, stat_ref, mine_ref, other_ref, w_ref, acc_ref, proj_ref
    )
    scale_ref[...] = scale
    folded = jnp.zeros((tokens, HD), F32)
    masks = [listed(ints_ref, 1, b, (tokens, BLK), 0) for b in range(tokens // BLK)]
    for h in range(local // HD):
        at = h * HD
        query = proj_ref[:, at : at + HD]
        key_in = proj_ref[:, local + at : local + at + HD]
        value = proj_ref[:, 2 * local + at : 2 * local + at + HD]
        upstream = c_ref[:, at : at + HD]
        for b, mask in enumerate(masks):
            cols = slice(b * BLK, (b + 1) * BLK)
            probs = softmax(contract(key_in, query[cols], 1, 1), mask, 0)
            grad_p = contract(value, upstream[cols], 1, 1)
            inner = jnp.sum(probs * grad_p, axis=0, keepdims=True)
            p_ref[:, cols] = probs.astype(BF16)
            s_ref[:, cols] = (probs * (grad_p - inner) * (1.0 / math.sqrt(HD))).astype(BF16)
        grad_s = s_ref[...]
        parts = (
            contract(grad_s, key_in, 0, 0),
            jnp.dot(grad_s, query, preferred_element_type=F32),
            jnp.dot(p_ref[...], upstream, preferred_element_type=F32),
        )
        for j, part in enumerate(parts):
            cols = slice(j * local + at, j * local + at + HD)
            grads = (scale * part).astype(BF16)
            out_ref[:tokens, cols] = grads
            folded = folded + grads.astype(F32) * acc_ref[:, cols]
    out_ref[tokens:, :] = stat_rows(row_sums(folded), out_ref.shape[1])


def input_grad_kernel(places, ints_ref, mine_ref, other_ref, w_mine_ref, w_other_ref, *out_refs):
    tokens = mine_ref.shape[0] - STAT
    local = out_refs[0].shape[1]
    grads = jnp.concatenate([mine_ref[:tokens, :], other_ref[:tokens, :]], axis=1)
    totals = stat_row(mine_ref[tokens:, :].astype(F32) + other_ref[tokens:, :].astype(F32), tokens)
    stats = stat_rows(totals, local)
    for place, ref in zip(places, out_refs):
        rows = pl.ds(pl.multiple_of(ints_ref[50 + place] * local, local), local)
        w_all = jnp.concatenate(
            [w[j, rows, :] for w in (w_mine_ref, w_other_ref) for j in range(3)], axis=1
        )
        ref[:tokens, :] = contract(grads, w_all, 1, 1).astype(BF16)
        ref[tokens:, :] = stats


def weight_grad_kernel(ints_ref, mine_ref, other_ref, more_ref, rest_ref, g_ref, out_ref):
    tokens = g_ref.shape[0] - STAT
    local = mine_ref.shape[2]
    side = ints_ref[66]
    step = pl.program_id(0)
    grads = g_ref[:tokens, :]

    def add(ref, at, i):
        part = contract(ref[i, :tokens, :], grads, 0, 0)
        for j in range(3):
            out_ref[j, pl.ds(pl.multiple_of(at * local, local), local), :] = part[
                :, j * local : (j + 1) * local
            ].astype(BF16)

    half = mine_ref.shape[0]

    @pl.when(step < half)
    def _():
        add(mine_ref, side, step)
        add(other_ref, 1 - side, step)

    @pl.when(step >= half)
    def _():
        add(more_ref, side, step - half)
        add(rest_ref, 1 - side, step - half)


def weight_grad(ints, blocks, grads):
    chips, rows, local = 2 * blocks[0].shape[0], *blocks[0].shape[1:]
    whole = lambda a: pl.BlockSpec(a.shape, lambda d, ints: (0,) * a.ndim)
    return pl.pallas_call(
        weight_grad_kernel,
        out_shape=jax.ShapeDtypeStruct((3, 2 * chips * local, local), BF16),
        grid_spec=pltpu.PrefetchScalarGridSpec(
            num_scalar_prefetch=1,
            grid=(chips,),
            in_specs=[whole(a) for a in (*blocks, grads)],
            out_specs=pl.BlockSpec((3, 2 * local, local), lambda d, ints: (0, ints[67 + d], 0)),
        ),
        compiler_params=pltpu.CompilerParams(vmem_limit_bytes=VMEM_BYTES),
        cost_estimate=cost(7.0),
        name="weight_grad",
    )(ints, *blocks, grads)


def finish_kernel(*refs):
    blocks, (x_ref, c_ref, gain_ref, scale_ref, dx_ref, gg_ref) = refs[:CHIPS], refs[CHIPS:]
    tokens, local = x_ref.shape
    own_in = blocks[0][:tokens, :].astype(F32)
    stats = blocks[0][tokens:, :].astype(F32)
    for ref in blocks[1:]:
        own_in = own_in + ref[:tokens, :].astype(F32)
        stats = stats + ref[tokens:, :].astype(F32)
    total = as_column(stat_row(stats, tokens))
    scale = scale_ref[...]
    factor = scale * scale * total / (2 * CHIPS * local)
    x_wide = x_ref[...].astype(F32)
    for start in range(0, local, HD):
        cols = slice(start, start + HD)
        grad_x = c_ref[:, cols].astype(F32) + gain_ref[:, cols] * own_in[:, cols]
        dx_ref[:, cols] = (grad_x - factor * x_wide[:, cols]).astype(BF16)
    gg_ref[...] = jnp.sum(x_wide * own_in, axis=0, keepdims=True)


def cost(us):
    return pl.CostEstimate(flops=int(us * 1.1e9), transcendentals=0, bytes_accessed=0)


def plain_call(kernel, out_shape, name, us, *args, scratch=()):
    vmem = pl.BlockSpec(memory_space=pltpu.VMEM)
    specs = [
        pl.BlockSpec(memory_space=pltpu.SMEM) if a.dtype == jnp.int32 else vmem for a in args
    ]
    return pl.pallas_call(
        kernel,
        out_shape=out_shape,
        in_specs=specs,
        out_specs=jax.tree.map(lambda s: vmem, out_shape),
        scratch_shapes=list(scratch),
        compiler_params=pltpu.CompilerParams(vmem_limit_bytes=VMEM_BYTES),
        cost_estimate=cost(us),
        name=name,
    )(*args)


def to_chip(block, distance):
    route = [(i, ((i >> 1) ^ distance) << 1 | (i & 1)) for i in range(2 * CHIPS)]
    return lax.ppermute(block, "fsdp", route)


def to_core(block):
    return lax.ppermute(block, "fsdp", [(i, i ^ 1) for i in range(2 * CHIPS)])


def shifted(block, axis, distance):
    count = lax.axis_size(axis)
    return lax.ppermute(block, axis, [((i - distance) % count, i) for i in range(count)])


NEAR = (0, 4, 1, 3)
FAR = (2, 5, 7, 6)
SPLIT = 208
tie = lax.optimization_barrier


def near(block):
    return [block] + [to_chip(block, d) for d in NEAR[1:]]


def far(blocks):
    _, by_x, by_1, by_3 = blocks
    return to_chip(by_3, 1), to_chip(by_1, 4), to_chip(by_x, 3)


def last(blocks):
    at_2, _, at_7 = blocks
    return jnp.concatenate([to_chip(at_2[:SPLIT], 4), to_chip(at_7[SPLIT:], 1)])


def on_device(x_fwd, x_saved, cotangent, qkv_weight, gain, block_lists, plan):
    forward_in = x_fwd[0]
    saved_in = x_saved[0]
    upstream = cotangent[0]
    weight = jnp.transpose(qkv_weight[0], (1, 0, 2))
    tokens, local = forward_in.shape
    me = lax.axis_index("fsdp").astype(jnp.int32)
    chip, side = me // 2, me % 2
    apart = jnp.array(NEAR + FAR, dtype=jnp.int32) ^ chip
    ints = jnp.concatenate(
        [
            block_lists.reshape(-1),
            plan.reshape(-1),
            apart * 2 + side,
            apart * 2 + 1 - side,
            side[None],
            apart,
        ]
    )
    block = jax.ShapeDtypeStruct((tokens + STAT, local), BF16)
    wide = jax.ShapeDtypeStruct((tokens, 3 * local), F32)
    stat = jax.ShapeDtypeStruct((STAT, local), F32)
    narrow = jax.ShapeDtypeStruct((tokens, local), BF16)
    proj = pltpu.VMEM((tokens, 3 * local), BF16)

    pay_bwd = plain_call(pack_kernel, block, "pack_bwd", 1.0, saved_in, gain)
    pay_fwd = plain_call(pack_kernel, block, "pack_fwd", 1.0, forward_in, gain)
    w_other = to_core(weight)

    near_bwd = near(pay_bwd)
    mine_a = jnp.stack(near_bwd)
    other_a = to_core(mine_a)
    far_bwd = far(near_bwd)
    first, first_stat = plain_call(
        first_kernel, (wide, stat), "first_bwd", 2.5, ints, mine_a, other_a, weight
    )
    far_bwd, w_other, pay_fwd = tie((far_bwd, w_other, pay_fwd))
    mine_b = jnp.stack([*far_bwd, last(far_bwd)])
    near_fwd = near(pay_fwd)
    other_b = to_core(mine_b)
    grads, scale = plain_call(
        backward_kernel,
        (
            jax.ShapeDtypeStruct((tokens + STAT, 3 * local), BF16),
            jax.ShapeDtypeStruct((tokens, HD), F32),
        ),
        "backward",
        6.0,
        ints,
        first,
        first_stat,
        mine_b,
        other_b,
        weight,
        upstream,
        scratch=[
            pltpu.VMEM((tokens, 3 * local), F32),
            proj,
            pltpu.VMEM((tokens, tokens), BF16),
            pltpu.VMEM((tokens, tokens), BF16),
        ],
    )
    far_fwd = far(near_fwd)
    grads_other = to_core(grads)
    gone = []
    for name, places in (("input_grad_far", (7, 6, 5, 4)), ("input_grad_near", (1, 2, 3, 0))):
        parts = plain_call(
            functools.partial(input_grad_kernel, places),
            [block] * 4,
            name,
            2.0,
            ints,
            grads,
            grads_other,
            weight,
            w_other,
        )
        for place, part in zip(places, parts):
            gone.append(to_chip(part, (NEAR + FAR)[place]) if place else part)

    mine_fa = jnp.stack(near_fwd)
    mine_fb = jnp.stack([*far_fwd, last(far_fwd)])
    other_fa, other_fb = to_core(mine_fa), to_core(mine_fb)
    first_f, stat_f = plain_call(
        first_kernel, (wide, stat), "first_fwd", 2.5, ints, mine_fa, other_fa, weight
    )
    result = plain_call(
        forward_kernel,
        narrow,
        "forward",
        4.0,
        ints,
        first_f,
        stat_f,
        mine_fb,
        other_fb,
        weight,
        forward_in,
        scratch=[proj],
    )
    sent_on = shifted(result, "section", 1)
    grad_w = weight_grad(ints, (mine_a, other_a, mine_b, other_b), grads)
    grad_x, grad_gain = plain_call(
        finish_kernel,
        (narrow, jax.ShapeDtypeStruct((1, local), F32)),
        "finish",
        1.0,
        *gone,
        saved_in,
        upstream,
        gain,
        scale,
    )
    sent_back = shifted(grad_x, "section", -1)
    return (sent_on[None], sent_back[None], jnp.transpose(grad_w, (1, 0, 2))[None], grad_gain)


def solution(mesh):
    in_specs = (
        P("section", None, "fsdp"),
        P("section", None, "fsdp"),
        P("section", None, "fsdp"),
        P("section", None, None, "fsdp"),
        P("section", "fsdp"),
        P(),
        P("section", None),
    )
    out_specs = (
        P("section", None, "fsdp"),
        P("section", None, "fsdp"),
        P("section", None, None, "fsdp"),
        P("section", "fsdp"),
    )
    return jax.shard_map(
        on_device, mesh=mesh, in_specs=in_specs, out_specs=out_specs, check_vma=False
    )
```

```python
import functools
import math

import jax
import jax.numpy as jnp
from jax import lax
from jax.experimental import pallas as pl
from jax.experimental.pallas import tpu as pltpu
from jax.sharding import PartitionSpec as P

HD = 128
BLK = 128
EPS = 1e-05
STAT = 16
CHIPS = 8
F32 = jnp.float32
BF16 = jnp.bfloat16
VMEM_BYTES = 16 << 20


def pieces(row):
    high = row.astype(BF16).astype(F32)
    rest = row - high
    mid = rest.astype(BF16).astype(F32)
    return high, mid, rest - mid


def stat_rows(row, width):
    span = row.shape[1]
    index = lax.broadcasted_iota(jnp.int32, (STAT, width), 0)
    out = jnp.zeros((STAT, width), F32)
    for i, part in enumerate(pieces(row)):
        for j, start in enumerate(range(0, span, width)):
            held = part[:, start : start + width]
            if held.shape[1] < width:
                held = jnp.concatenate(
                    [held, jnp.zeros((1, width - held.shape[1]), F32)], axis=1
                )
            out = jnp.where(index == 3 * j + i, jnp.broadcast_to(held, (STAT, width)), out)
    return out.astype(BF16)


def stat_row(rows, span):
    width = rows.shape[1]
    parts = []
    for j, start in enumerate(range(0, span, width)):
        part = rows[3 * j : 3 * j + 1] + rows[3 * j + 1 : 3 * j + 2] + rows[3 * j + 2 : 3 * j + 3]
        parts.append(part[:, : min(width, span - start)])
    return parts[0] if len(parts) == 1 else jnp.concatenate(parts, axis=1)


def as_column(row):
    return jnp.transpose(jnp.broadcast_to(row, (HD, row.shape[1])))


def row_sums(folded):
    return jnp.sum(jnp.transpose(folded), axis=0, keepdims=True)


def pack_kernel(x_ref, gain_ref, out_ref):
    tokens = x_ref.shape[0]
    wide = x_ref[...].astype(F32)
    out_ref[:tokens, :] = (wide * gain_ref[...]).astype(BF16)
    squares = wide * wide
    folded = squares[:, :HD]
    for start in range(HD, squares.shape[1], HD):
        folded = folded + squares[:, start : start + HD]
    out_ref[tokens:, :] = stat_rows(row_sums(folded), out_ref.shape[1])


def listed(ints_ref, which, b, shape, dim):
    z = ints_ref[48 + which]
    block = lax.shift_right_logical(
        lax.broadcasted_iota(jnp.int32, shape, dim), BLK.bit_length() - 1
    )
    return (block == ints_ref[z * 6 + b * 2]) | (block == ints_ref[z * 6 + b * 2 + 1])


def contract(left, right, left_dim, right_dim):
    return lax.dot_general(
        left, right, (((left_dim,), (right_dim,)), ((), ())), preferred_element_type=F32
    )


def softmax(scores, mask, axis):
    scores = jnp.where(mask, scores * (1.0 / math.sqrt(HD)), -1e30)
    expd = jnp.exp(scores - jnp.max(scores, axis=axis, keepdims=True))
    return expd * (1.0 / jnp.sum(expd, axis=axis, keepdims=True))


def partial_product(ints_ref, at, mine_ref, other_ref, w_ref, tokens):
    count, _, local = mine_ref.shape
    both = [(ref, i) for i in range(count) for ref in (mine_ref, other_ref)]
    x_all = jnp.concatenate([ref[i, :tokens, :] for ref, i in both], axis=1)
    places = [ints_ref[50 + side * 8 + at + i] for i in range(count) for side in range(2)]
    parts = []
    for j in range(3):
        w_all = jnp.concatenate(
            [w_ref[j, pl.ds(pl.multiple_of(p * local, local), local), :] for p in places], axis=0
        )
        parts.append(jnp.dot(x_all, w_all, preferred_element_type=F32))
    stats = sum(ref[i, tokens:, :].astype(F32) for ref, i in both)
    return parts, stats


def first_kernel(ints_ref, mine_ref, other_ref, w_ref, acc_ref, stat_ref):
    tokens = acc_ref.shape[0]
    local = mine_ref.shape[2]
    parts, stats = partial_product(ints_ref, 0, mine_ref, other_ref, w_ref, tokens)
    for j, part in enumerate(parts):
        acc_ref[:, j * local : (j + 1) * local] = part
    stat_ref[...] = stats


def finish_product(ints_ref, first_ref, stat_ref, mine_ref, other_ref, w_ref, acc_ref, proj_ref):
    tokens = first_ref.shape[0]
    local = mine_ref.shape[2]
    parts, stats = partial_product(ints_ref, 4, mine_ref, other_ref, w_ref, tokens)
    width = 2 * CHIPS * local
    scale = lax.rsqrt(as_column(stat_row(stat_ref[...] + stats, tokens)) / width + EPS)
    for j, part in enumerate(parts):
        for start in range(0, local, HD):
            cols = slice(j * local + start, j * local + start + HD)
            whole = first_ref[:, cols] + part[:, start : start + HD]
            if acc_ref is not None:
                acc_ref[:, cols] = whole
            proj_ref[:, cols] = (scale * whole).astype(BF16)
    return scale


def forward_kernel(
    ints_ref, first_ref, stat_ref, mine_ref, other_ref, w_ref, x_ref, out_ref, proj_ref
):
    tokens, local = x_ref.shape
    finish_product(ints_ref, first_ref, stat_ref, mine_ref, other_ref, w_ref, None, proj_ref)
    for b in range(tokens // BLK):
        rows = slice(b * BLK, (b + 1) * BLK)
        mask = listed(ints_ref, 0, b, (BLK, tokens), 1)
        for h in range(local // HD):
            at = h * HD
            key_in = proj_ref[:, local + at : local + at + HD]
            value = proj_ref[:, 2 * local + at : 2 * local + at + HD]
            scores = contract(proj_ref[rows, at : at + HD], key_in, 1, 1)
            probs = softmax(scores, mask, 1)
            attn = jnp.dot(probs.astype(BF16), value, preferred_element_type=F32)
            out_ref[rows, at : at + HD] = (x_ref[rows, at : at + HD].astype(F32) + attn).astype(
                BF16
            )


def backward_kernel(
    ints_ref,
    first_ref,
    stat_ref,
    mine_ref,
    other_ref,
    w_ref,
    c_ref,
    out_ref,
    scale_ref,
    acc_ref,
    proj_ref,
    p_ref,
    s_ref,
):
    tokens, local = c_ref.shape
    scale = finish_product(
        ints_ref, first_ref, stat_ref, mine_ref, other_ref, w_ref, acc_ref, proj_ref
    )
    scale_ref[...] = scale
    folded = jnp.zeros((tokens, HD), F32)
    masks = [listed(ints_ref, 1, b, (tokens, BLK), 0) for b in range(tokens // BLK)]
    for h in range(local // HD):
        at = h * HD
        query = proj_ref[:, at : at + HD]
        key_in = proj_ref[:, local + at : local + at + HD]
        value = proj_ref[:, 2 * local + at : 2 * local + at + HD]
        upstream = c_ref[:, at : at + HD]
        for b, mask in enumerate(masks):
            cols = slice(b * BLK, (b + 1) * BLK)
            probs = softmax(contract(key_in, query[cols], 1, 1), mask, 0)
            grad_p = contract(value, upstream[cols], 1, 1)
            inner = jnp.sum(probs * grad_p, axis=0, keepdims=True)
            p_ref[:, cols] = probs.astype(BF16)
            s_ref[:, cols] = (probs * (grad_p - inner) * (1.0 / math.sqrt(HD))).astype(BF16)
        grad_s = s_ref[...]
        parts = (
            contract(grad_s, key_in, 0, 0),
            jnp.dot(grad_s, query, preferred_element_type=F32),
            jnp.dot(p_ref[...], upstream, preferred_element_type=F32),
        )
        for j, part in enumerate(parts):
            cols = slice(j * local + at, j * local + at + HD)
            grads = (scale * part).astype(BF16)
            out_ref[:tokens, cols] = grads
            folded = folded + grads.astype(F32) * acc_ref[:, cols]
    out_ref[tokens:, :] = stat_rows(row_sums(folded), out_ref.shape[1])


def input_grad_kernel(places, ints_ref, mine_ref, other_ref, w_mine_ref, w_other_ref, *out_refs):
    tokens = mine_ref.shape[0] - STAT
    local = w_mine_ref.shape[2]
    grads = jnp.concatenate([mine_ref[:tokens, :], other_ref[:tokens, :]], axis=1)
    totals = stat_row(mine_ref[tokens:, :].astype(F32) + other_ref[tokens:, :].astype(F32), tokens)
    stats = stat_rows(totals, local)
    for place, ref in zip(places, out_refs):
        rows = pl.ds(pl.multiple_of(ints_ref[50 + place] * local, local), local)
        w_all = jnp.concatenate(
            [w[j, rows, :] for w in (w_mine_ref, w_other_ref) for j in range(3)], axis=1
        )
        ref[:tokens, :] = contract(grads, w_all, 1, 1).astype(ref.dtype)
        if ref.shape[0] > tokens:
            ref[tokens:, :] = stats
    if len(out_refs) > len(places):
        out_refs[-1][...] = stats


def add_kernel(pair_ref, *refs):
    count = len(refs) // 3
    pair = pair_ref[...].astype(F32)
    for part, came, out in zip(refs[:count], refs[count : 2 * count], refs[2 * count :]):
        tokens = part.shape[0]
        out[:tokens, :] = (part[...] + came[:tokens, :].astype(F32)).astype(BF16)
        total = stat_row(pair + came[tokens:, :].astype(F32), tokens)
        out[tokens:, :] = stat_rows(total, out.shape[1])


def weight_grad_kernel(
    ints_ref, mine_ref, other_ref, more_ref, rest_ref, g_ref, out_ref, buf_ref, sem_ref
):
    tokens = g_ref.shape[0] - STAT
    half, _, local = mine_ref.shape
    side = ints_ref[66]
    grads = g_ref[:tokens, :]

    def copy(piece, j, row):
        return pltpu.make_async_copy(
            buf_ref.at[piece, j], out_ref.at[j, pl.ds(row, local), :], sem_ref.at[piece, j]
        )

    copies = []
    for s, pair in enumerate(((mine_ref, other_ref), (more_ref, rest_ref))):
        for i in range(half):
            for k, ref in enumerate(pair):
                piece = (s * half + i) * 2 + k
                place = ints_ref[67 + s * half + i] * 2 + (side if k == 0 else 1 - side)
                part = contract(ref[i, :tokens, :], grads, 0, 0)
                for j in range(3):
                    buf_ref[piece, j] = part[:, j * local : (j + 1) * local].astype(BF16)
                    copies.append(copy(piece, j, pl.multiple_of(place * local, local)))
                    copies[-1].start()
    for held in copies:
        held.wait()


def weight_grad(ints, blocks, grads):
    chips, rows, local = 2 * blocks[0].shape[0], *blocks[0].shape[1:]
    vmem = pl.BlockSpec(memory_space=pltpu.VMEM)
    return pl.pallas_call(
        weight_grad_kernel,
        out_shape=jax.ShapeDtypeStruct((3, 2 * chips * local, local), BF16),
        in_specs=[pl.BlockSpec(memory_space=pltpu.SMEM), *([vmem] * 5)],
        out_specs=pl.BlockSpec(memory_space=pltpu.HBM),
        scratch_shapes=[
            pltpu.VMEM((2 * chips, 3, local, local), BF16),
            pltpu.SemaphoreType.DMA((2 * chips, 3)),
        ],
        compiler_params=pltpu.CompilerParams(vmem_limit_bytes=VMEM_BYTES),
        cost_estimate=cost(5.0),
        name="weight_grad",
    )(ints, *blocks, grads)


def finish_kernel(own_ref, pair_ref, *refs):
    blocks, (x_ref, c_ref, gain_ref, scale_ref, dx_ref, gg_ref) = refs[:-6], refs[-6:]
    tokens, local = x_ref.shape
    own_in = own_ref[...]
    stats = pair_ref[...].astype(F32)
    for ref in blocks:
        own_in = own_in + ref[:tokens, :].astype(F32)
        stats = stats + ref[tokens:, :].astype(F32)
    total = as_column(stat_row(stats, tokens))
    scale = scale_ref[...]
    factor = scale * scale * total / (2 * CHIPS * local)
    x_wide = x_ref[...].astype(F32)
    for start in range(0, local, HD):
        cols = slice(start, start + HD)
        grad_x = c_ref[:, cols].astype(F32) + gain_ref[:, cols] * own_in[:, cols]
        dx_ref[:, cols] = (grad_x - factor * x_wide[:, cols]).astype(BF16)
    gg_ref[...] = jnp.sum(x_wide * own_in, axis=0, keepdims=True)


def cost(us):
    return pl.CostEstimate(flops=int(us * 1.1e9), transcendentals=0, bytes_accessed=0)


def plain_call(kernel, out_shape, name, us, *args, scratch=(), held=True):
    vmem = pl.BlockSpec(memory_space=pltpu.VMEM) if held else pl.BlockSpec()
    specs = [
        pl.BlockSpec(memory_space=pltpu.SMEM) if a.dtype == jnp.int32 else vmem for a in args
    ]
    return pl.pallas_call(
        kernel,
        out_shape=out_shape,
        in_specs=specs,
        out_specs=jax.tree.map(lambda s: vmem, out_shape),
        scratch_shapes=list(scratch),
        compiler_params=pltpu.CompilerParams(vmem_limit_bytes=VMEM_BYTES),
        cost_estimate=cost(us),
        name=name,
    )(*args)


def to_chip(block, distance):
    route = [(i, ((i >> 1) ^ distance) << 1 | (i & 1)) for i in range(2 * CHIPS)]
    return lax.ppermute(block, "fsdp", route)


def to_core(block):
    return lax.ppermute(block, "fsdp", [(i, i ^ 1) for i in range(2 * CHIPS)])


def shifted(block, axis, distance):
    count = lax.axis_size(axis)
    return lax.ppermute(block, axis, [((i - distance) % count, i) for i in range(count)])


NEAR = (0, 4, 1, 3)
FAR = (2, 5, 7, 6)
tie = lax.optimization_barrier


def near(block):
    return [block] + [to_chip(block, d) for d in NEAR[1:]]


def far(blocks):
    _, by_x, by_1, by_3 = blocks
    return [to_chip(by_3, 1), to_chip(by_1, 4), to_chip(by_x, 3)]


def on_device(x_fwd, x_saved, cotangent, qkv_weight, gain, block_lists, plan):
    forward_in = x_fwd[0]
    saved_in = x_saved[0]
    upstream = cotangent[0]
    weight = jnp.transpose(qkv_weight[0], (1, 0, 2))
    tokens, local = forward_in.shape
    me = lax.axis_index("fsdp").astype(jnp.int32)
    chip, side = me // 2, me % 2
    apart = jnp.array(NEAR + FAR, dtype=jnp.int32) ^ chip
    ints = jnp.concatenate(
        [
            block_lists.reshape(-1),
            plan.reshape(-1),
            apart * 2 + side,
            apart * 2 + 1 - side,
            side[None],
            apart,
        ]
    )
    block = jax.ShapeDtypeStruct((tokens + STAT, local), BF16)
    wide = jax.ShapeDtypeStruct((tokens, 3 * local), F32)
    stat = jax.ShapeDtypeStruct((STAT, local), F32)
    narrow = jax.ShapeDtypeStruct((tokens, local), BF16)
    proj = pltpu.VMEM((tokens, 3 * local), BF16)

    pay_bwd = plain_call(pack_kernel, block, "pack_bwd", 1.0, saved_in, gain, held=False)
    pay_fwd = plain_call(pack_kernel, block, "pack_fwd", 1.0, forward_in, gain, held=False)
    w_other = to_core(weight)

    near_bwd = near(pay_bwd)
    pay_bwd, pay_fwd = tie((pay_bwd, pay_fwd))
    last_bwd = to_chip(pay_bwd, FAR[-1])
    near_bwd, pay_fwd = tie((near_bwd, pay_fwd))
    mine_a = jnp.stack(near_bwd)
    other_a = to_core(mine_a)
    far_bwd = far(near_bwd)
    first, first_stat = plain_call(
        first_kernel, (wide, stat), "first_bwd", 2.5, ints, mine_a, other_a, weight
    )
    last_bwd, first, w_other, pay_fwd = tie((last_bwd, first, w_other, pay_fwd))
    mine_b = jnp.stack([*far_bwd, last_bwd])
    other_b = to_core(mine_b)
    near_fwd, last_fwd = near(pay_fwd), to_chip(pay_fwd, FAR[-1])
    grads, scale = plain_call(
        backward_kernel,
        (
            jax.ShapeDtypeStruct((tokens + STAT, 3 * local), BF16),
            jax.ShapeDtypeStruct((tokens, HD), F32),
        ),
        "backward",
        6.0,
        ints,
        first,
        first_stat,
        mine_b,
        other_b,
        weight,
        upstream,
        scratch=[
            pltpu.VMEM((tokens, 3 * local), F32),
            proj,
            pltpu.VMEM((tokens, tokens), BF16),
            pltpu.VMEM((tokens, tokens), BF16),
        ],
    )
    near_fwd, last_fwd, grads = tie((near_fwd, last_fwd, grads))
    grads_other = to_core(grads)
    far_fwd = far(near_fwd)

    def input_grads(places, grads, name, shapes):
        return plain_call(
            functools.partial(input_grad_kernel, places),
            shapes,
            name,
            3.5,
            ints,
            grads,
            grads_other,
            weight,
            w_other,
        )

    for_2, for_5, for_7, for_6 = input_grads((4, 5, 6, 7), grads, "input_grad_far", [block] * 4)
    alone = jax.ShapeDtypeStruct((tokens, local), F32)
    later, for_7 = tie((grads, for_7))
    *parts, own, pair = input_grads(
        (1, 2, 3, 0),
        later,
        "input_grad_near",
        [alone] * 4 + [jax.ShapeDtypeStruct((STAT, local), BF16)],
    )
    came = [to_chip(for_7, 3), to_chip(for_5, 4), to_chip(for_2, 1)]
    direct = to_chip(for_6, 6)
    far_fwd, near_fwd, pair = tie((far_fwd, near_fwd, pair))
    mine_fa = jnp.stack(near_fwd)
    other_fa = to_core(mine_fa)
    mine_fb = jnp.stack([*far_fwd, last_fwd])
    other_fb = to_core(mine_fb)
    first_f, stat_f = plain_call(
        first_kernel, (wide, stat), "first_fwd", 2.5, ints, mine_fa, other_fa, weight
    )
    came, first_f = tie((came, first_f))
    sums = plain_call(add_kernel, [block] * 3, "add", 1.0, pair, *parts, *came)
    gone = [to_chip(part, d) for part, d in zip(sums, NEAR[1:])] + [direct]
    result = plain_call(
        forward_kernel,
        narrow,
        "forward",
        4.5,
        ints,
        first_f,
        stat_f,
        mine_fb,
        other_fb,
        weight,
        forward_in,
        scratch=[proj],
    )
    sent_on = shifted(result, "section", 1)
    gone, result = tie((gone, result))
    grad_w = weight_grad(ints, (mine_a, other_a, mine_b, other_b), grads)
    grad_x, grad_gain = plain_call(
        finish_kernel,
        (narrow, jax.ShapeDtypeStruct((1, local), F32)),
        "finish",
        1.0,
        own,
        pair,
        *gone,
        saved_in,
        upstream,
        gain,
        scale,
    )
    sent_back = shifted(grad_x, "section", -1)
    return (sent_on[None], sent_back[None], jnp.transpose(grad_w, (1, 0, 2))[None], grad_gain)


def solution(mesh):
    in_specs = (
        P("section", None, "fsdp"),
        P("section", None, "fsdp"),
        P("section", None, "fsdp"),
        P("section", None, None, "fsdp"),
        P("section", "fsdp"),
        P(),
        P("section", None),
    )
    out_specs = (
        P("section", None, "fsdp"),
        P("section", None, "fsdp"),
        P("section", None, None, "fsdp"),
        P("section", "fsdp"),
    )
    return jax.shard_map(
        on_device, mesh=mesh, in_specs=in_specs, out_specs=out_specs, check_vma=False
    )
```

```python
import functools
import math

import jax
import jax.numpy as jnp
from jax import lax
from jax.experimental import pallas as pl
from jax.experimental.pallas import tpu as pltpu
from jax.sharding import PartitionSpec as P

HD = 128
BLK = 128
EPS = 1e-05
STAT = 16
CHIPS = 8
F32 = jnp.float32
BF16 = jnp.bfloat16
VMEM_BYTES = 16 << 20


def pieces(row):
    high = row.astype(BF16).astype(F32)
    rest = row - high
    mid = rest.astype(BF16).astype(F32)
    return high, mid, rest - mid


def stat_rows(row, width):
    span = row.shape[1]
    index = lax.broadcasted_iota(jnp.int32, (STAT, width), 0)
    out = jnp.zeros((STAT, width), F32)
    for i, part in enumerate(pieces(row)):
        for j, start in enumerate(range(0, span, width)):
            held = part[:, start : start + width]
            if held.shape[1] < width:
                held = jnp.concatenate(
                    [held, jnp.zeros((1, width - held.shape[1]), F32)], axis=1
                )
            out = jnp.where(index == 3 * j + i, jnp.broadcast_to(held, (STAT, width)), out)
    return out.astype(BF16)


def stat_row(rows, span):
    width = rows.shape[1]
    parts = []
    for j, start in enumerate(range(0, span, width)):
        part = rows[3 * j : 3 * j + 1] + rows[3 * j + 1 : 3 * j + 2] + rows[3 * j + 2 : 3 * j + 3]
        parts.append(part[:, : min(width, span - start)])
    return parts[0] if len(parts) == 1 else jnp.concatenate(parts, axis=1)


def as_column(row):
    return jnp.transpose(jnp.broadcast_to(row, (HD, row.shape[1])))


def row_sums(folded):
    return jnp.sum(jnp.transpose(folded), axis=0, keepdims=True)


def pack_kernel(x_hbm, gain_hbm, out_ref, x_ref, gain_ref, sem_ref):
    copies = [
        pltpu.make_async_copy(x_hbm, x_ref, sem_ref.at[0]),
        pltpu.make_async_copy(gain_hbm, gain_ref, sem_ref.at[1]),
    ]
    for held in copies:
        held.start()
    for held in copies:
        held.wait()
    tokens = x_ref.shape[0]
    wide = x_ref[...].astype(F32)
    out_ref[:tokens, :] = (wide * gain_ref[...]).astype(BF16)
    squares = wide * wide
    folded = squares[:, :HD]
    for start in range(HD, squares.shape[1], HD):
        folded = folded + squares[:, start : start + HD]
    out_ref[tokens:, :] = stat_rows(row_sums(folded), out_ref.shape[1])


def listed(ints_ref, which, b, shape, dim):
    z = ints_ref[48 + which]
    block = lax.shift_right_logical(
        lax.broadcasted_iota(jnp.int32, shape, dim), BLK.bit_length() - 1
    )
    return (block == ints_ref[z * 6 + b * 2]) | (block == ints_ref[z * 6 + b * 2 + 1])


def contract(left, right, left_dim, right_dim):
    return lax.dot_general(
        left, right, (((left_dim,), (right_dim,)), ((), ())), preferred_element_type=F32
    )


def softmax(scores, mask, axis):
    scores = jnp.where(mask, scores * (1.0 / math.sqrt(HD)), -1e30)
    expd = jnp.exp(scores - jnp.max(scores, axis=axis, keepdims=True))
    return expd * (1.0 / jnp.sum(expd, axis=axis, keepdims=True))


def partial_product(ints_ref, at, mine_ref, other_ref, w_ref, tokens):
    count, _, local = mine_ref.shape
    both = [(ref, i) for i in range(count) for ref in (mine_ref, other_ref)]
    x_all = jnp.concatenate([ref[i, :tokens, :] for ref, i in both], axis=1)
    places = [ints_ref[50 + side * 8 + at + i] for i in range(count) for side in range(2)]
    parts = []
    for j in range(3):
        w_all = jnp.concatenate(
            [w_ref[j, pl.ds(pl.multiple_of(p * local, local), local), :] for p in places], axis=0
        )
        parts.append(jnp.dot(x_all, w_all, preferred_element_type=F32))
    stats = sum(ref[i, tokens:, :].astype(F32) for ref, i in both)
    return parts, stats


def first_kernel(ints_ref, mine_ref, other_ref, w_ref, acc_ref, stat_ref):
    tokens = acc_ref.shape[0]
    local = mine_ref.shape[2]
    parts, stats = partial_product(ints_ref, 0, mine_ref, other_ref, w_ref, tokens)
    for j, part in enumerate(parts):
        acc_ref[:, j * local : (j + 1) * local] = part
    stat_ref[...] = stats


def finish_product(ints_ref, first_ref, stat_ref, mine_ref, other_ref, w_ref, acc_ref, proj_ref):
    tokens = first_ref.shape[0]
    local = mine_ref.shape[2]
    parts, stats = partial_product(ints_ref, 4, mine_ref, other_ref, w_ref, tokens)
    width = 2 * CHIPS * local
    scale = lax.rsqrt(as_column(stat_row(stat_ref[...] + stats, tokens)) / width + EPS)
    for j, part in enumerate(parts):
        for start in range(0, local, HD):
            cols = slice(j * local + start, j * local + start + HD)
            whole = first_ref[:, cols] + part[:, start : start + HD]
            if acc_ref is not None:
                acc_ref[:, cols] = whole
            proj_ref[:, cols] = (scale * whole).astype(BF16)
    return scale


def forward_kernel(
    ints_ref, first_ref, stat_ref, mine_ref, other_ref, w_ref, x_ref, out_ref, proj_ref
):
    tokens, local = x_ref.shape
    finish_product(ints_ref, first_ref, stat_ref, mine_ref, other_ref, w_ref, None, proj_ref)
    for b in range(tokens // BLK):
        rows = slice(b * BLK, (b + 1) * BLK)
        mask = listed(ints_ref, 0, b, (BLK, tokens), 1)
        for h in range(local // HD):
            at = h * HD
            key_in = proj_ref[:, local + at : local + at + HD]
            value = proj_ref[:, 2 * local + at : 2 * local + at + HD]
            scores = contract(proj_ref[rows, at : at + HD], key_in, 1, 1)
            probs = softmax(scores, mask, 1)
            attn = jnp.dot(probs.astype(BF16), value, preferred_element_type=F32)
            out_ref[rows, at : at + HD] = (x_ref[rows, at : at + HD].astype(F32) + attn).astype(
                BF16
            )


def backward_kernel(
    ints_ref,
    first_ref,
    stat_ref,
    mine_ref,
    other_ref,
    w_ref,
    c_ref,
    out_ref,
    scale_ref,
    acc_ref,
    proj_ref,
    p_ref,
    s_ref,
):
    tokens, local = c_ref.shape
    scale = finish_product(
        ints_ref, first_ref, stat_ref, mine_ref, other_ref, w_ref, acc_ref, proj_ref
    )
    scale_ref[...] = scale
    folded = jnp.zeros((tokens, HD), F32)
    masks = [listed(ints_ref, 1, b, (tokens, BLK), 0) for b in range(tokens // BLK)]
    for h in range(local // HD):
        at = h * HD
        query = proj_ref[:, at : at + HD]
        key_in = proj_ref[:, local + at : local + at + HD]
        value = proj_ref[:, 2 * local + at : 2 * local + at + HD]
        upstream = c_ref[:, at : at + HD]
        for b, mask in enumerate(masks):
            cols = slice(b * BLK, (b + 1) * BLK)
            probs = softmax(contract(key_in, query[cols], 1, 1), mask, 0)
            grad_p = contract(value, upstream[cols], 1, 1)
            inner = jnp.sum(probs * grad_p, axis=0, keepdims=True)
            p_ref[:, cols] = probs.astype(BF16)
            s_ref[:, cols] = (probs * (grad_p - inner) * (1.0 / math.sqrt(HD))).astype(BF16)
        grad_s = s_ref[...]
        parts = (
            contract(grad_s, key_in, 0, 0),
            jnp.dot(grad_s, query, preferred_element_type=F32),
            jnp.dot(p_ref[...], upstream, preferred_element_type=F32),
        )
        for j, part in enumerate(parts):
            cols = slice(j * local + at, j * local + at + HD)
            grads = (scale * part).astype(BF16)
            out_ref[:tokens, cols] = grads
            folded = folded + grads.astype(F32) * acc_ref[:, cols]
    out_ref[tokens:, :] = stat_rows(row_sums(folded), out_ref.shape[1])


def input_grad_kernel(places, ints_ref, mine_ref, other_ref, w_mine_ref, w_other_ref, *out_refs):
    tokens = mine_ref.shape[0] - STAT
    local = w_mine_ref.shape[2]
    grads = jnp.concatenate([mine_ref[:tokens, :], other_ref[:tokens, :]], axis=1)
    totals = stat_row(mine_ref[tokens:, :].astype(F32) + other_ref[tokens:, :].astype(F32), tokens)
    stats = stat_rows(totals, local)
    for place, ref in zip(places, out_refs):
        rows = pl.ds(pl.multiple_of(ints_ref[50 + place] * local, local), local)
        w_all = jnp.concatenate(
            [w[j, rows, :] for w in (w_mine_ref, w_other_ref) for j in range(3)], axis=1
        )
        ref[:tokens, :] = contract(grads, w_all, 1, 1).astype(ref.dtype)
        if ref.shape[0] > tokens:
            ref[tokens:, :] = stats
    if len(out_refs) > len(places):
        out_refs[-1][...] = stats


def add_kernel(pair_ref, *refs):
    count = len(refs) // 3
    pair = pair_ref[...].astype(F32)
    for part, came, out in zip(refs[:count], refs[count : 2 * count], refs[2 * count :]):
        tokens = part.shape[0]
        out[:tokens, :] = (part[...] + came[:tokens, :].astype(F32)).astype(BF16)
        total = stat_row(pair + came[tokens:, :].astype(F32), tokens)
        out[tokens:, :] = stat_rows(total, out.shape[1])


def weight_grad_kernel(
    ints_ref, mine_ref, other_ref, more_ref, rest_ref, g_ref, out_ref, buf_ref, sem_ref
):
    tokens = g_ref.shape[0] - STAT
    half, _, local = mine_ref.shape
    side = ints_ref[66]
    grads = g_ref[:tokens, :]

    def copy(piece, j, row):
        return pltpu.make_async_copy(
            buf_ref.at[piece, j], out_ref.at[j, pl.ds(row, local), :], sem_ref.at[piece, j]
        )

    copies = []
    for s, pair in enumerate(((mine_ref, other_ref), (more_ref, rest_ref))):
        for i in range(half):
            for k, ref in enumerate(pair):
                piece = (s * half + i) * 2 + k
                place = ints_ref[67 + s * half + i] * 2 + (side if k == 0 else 1 - side)
                part = contract(ref[i, :tokens, :], grads, 0, 0)
                for j in range(3):
                    buf_ref[piece, j] = part[:, j * local : (j + 1) * local].astype(BF16)
                    copies.append(copy(piece, j, pl.multiple_of(place * local, local)))
                    copies[-1].start()
    for held in copies:
        held.wait()


def weight_grad(ints, blocks, grads):
    chips, rows, local = 2 * blocks[0].shape[0], *blocks[0].shape[1:]
    vmem = pl.BlockSpec(memory_space=pltpu.VMEM)
    return pl.pallas_call(
        weight_grad_kernel,
        out_shape=jax.ShapeDtypeStruct((3, 2 * chips * local, local), BF16),
        in_specs=[pl.BlockSpec(memory_space=pltpu.SMEM), *([vmem] * 5)],
        out_specs=pl.BlockSpec(memory_space=pltpu.HBM),
        scratch_shapes=[
            pltpu.VMEM((2 * chips, 3, local, local), BF16),
            pltpu.SemaphoreType.DMA((2 * chips, 3)),
        ],
        compiler_params=pltpu.CompilerParams(vmem_limit_bytes=VMEM_BYTES),
        cost_estimate=cost(5.0),
        name="weight_grad",
    )(ints, *blocks, grads)


def finish_kernel(own_ref, pair_ref, *refs):
    blocks, (x_ref, c_ref, gain_ref, scale_ref, dx_ref, gg_ref) = refs[:-6], refs[-6:]
    tokens, local = x_ref.shape
    own_in = own_ref[...]
    stats = pair_ref[...].astype(F32)
    for ref in blocks:
        own_in = own_in + ref[:tokens, :].astype(F32)
        stats = stats + ref[tokens:, :].astype(F32)
    total = as_column(stat_row(stats, tokens))
    scale = scale_ref[...]
    factor = scale * scale * total / (2 * CHIPS * local)
    x_wide = x_ref[...].astype(F32)
    for start in range(0, local, HD):
        cols = slice(start, start + HD)
        grad_x = c_ref[:, cols].astype(F32) + gain_ref[:, cols] * own_in[:, cols]
        dx_ref[:, cols] = (grad_x - factor * x_wide[:, cols]).astype(BF16)
    gg_ref[...] = jnp.sum(x_wide * own_in, axis=0, keepdims=True)


def cost(us):
    return pl.CostEstimate(flops=int(us * 1.1e9), transcendentals=0, bytes_accessed=0)


def plain_call(kernel, out_shape, name, us, *args, scratch=(), held=True):
    vmem = pl.BlockSpec(memory_space=pltpu.VMEM) if held else pl.BlockSpec()
    specs = [
        pl.BlockSpec(memory_space=pltpu.SMEM) if a.dtype == jnp.int32 else vmem for a in args
    ]
    return pl.pallas_call(
        kernel,
        out_shape=out_shape,
        in_specs=specs,
        out_specs=jax.tree.map(lambda s: vmem, out_shape),
        scratch_shapes=list(scratch),
        compiler_params=pltpu.CompilerParams(vmem_limit_bytes=VMEM_BYTES),
        cost_estimate=cost(us),
        name=name,
    )(*args)


def pack(x, gain, name):
    tokens, local = x.shape
    hbm = pl.BlockSpec(memory_space=pltpu.HBM)
    return pl.pallas_call(
        pack_kernel,
        out_shape=jax.ShapeDtypeStruct((tokens + STAT, local), BF16),
        in_specs=[hbm, hbm],
        out_specs=pl.BlockSpec(memory_space=pltpu.VMEM),
        scratch_shapes=[
            pltpu.VMEM((tokens, local), BF16),
            pltpu.VMEM((1, local), F32),
            pltpu.SemaphoreType.DMA((2,)),
        ],
        compiler_params=pltpu.CompilerParams(vmem_limit_bytes=VMEM_BYTES),
        cost_estimate=cost(1.0),
        name=name,
    )(x, gain)


def to_chip(block, distance):
    route = [(i, ((i >> 1) ^ distance) << 1 | (i & 1)) for i in range(2 * CHIPS)]
    return lax.ppermute(block, "fsdp", route)


def to_core(block):
    return lax.ppermute(block, "fsdp", [(i, i ^ 1) for i in range(2 * CHIPS)])


def shifted(block, axis, distance):
    count = lax.axis_size(axis)
    return lax.ppermute(block, axis, [((i - distance) % count, i) for i in range(count)])


NEAR = (0, 4, 1, 3)
FAR = (2, 5, 7, 6)
tie = lax.optimization_barrier


def near(block):
    return [block] + [to_chip(block, d) for d in NEAR[1:]]


def far(blocks):
    _, by_x, by_1, by_3 = blocks
    return [to_chip(by_3, 1), to_chip(by_1, 4), to_chip(by_x, 3)]


def on_device(x_fwd, x_saved, cotangent, qkv_weight, gain, block_lists, plan):
    forward_in = x_fwd[0]
    saved_in = x_saved[0]
    upstream = cotangent[0]
    weight = jnp.transpose(qkv_weight[0], (1, 0, 2))
    tokens, local = forward_in.shape
    me = lax.axis_index("fsdp").astype(jnp.int32)
    chip, side = me // 2, me % 2
    apart = jnp.array(NEAR + FAR, dtype=jnp.int32) ^ chip
    ints = jnp.concatenate(
        [
            block_lists.reshape(-1),
            plan.reshape(-1),
            apart * 2 + side,
            apart * 2 + 1 - side,
            side[None],
            apart,
        ]
    )
    block = jax.ShapeDtypeStruct((tokens + STAT, local), BF16)
    wide = jax.ShapeDtypeStruct((tokens, 3 * local), F32)
    stat = jax.ShapeDtypeStruct((STAT, local), F32)
    narrow = jax.ShapeDtypeStruct((tokens, local), BF16)
    proj = pltpu.VMEM((tokens, 3 * local), BF16)

    pay_bwd = pack(saved_in, gain, "pack_bwd")
    pay_fwd = pack(forward_in, gain, "pack_fwd")
    w_other = to_core(weight)

    near_bwd = near(pay_bwd)
    pay_bwd, pay_fwd = tie((pay_bwd, pay_fwd))
    last_bwd = to_chip(pay_bwd, FAR[-1])
    near_bwd, pay_fwd = tie((near_bwd, pay_fwd))
    mine_a = jnp.stack(near_bwd)
    other_a = to_core(mine_a)
    far_bwd = far(near_bwd)
    first, first_stat = plain_call(
        first_kernel, (wide, stat), "first_bwd", 2.5, ints, mine_a, other_a, weight
    )
    last_bwd, first, w_other, pay_fwd = tie((last_bwd, first, w_other, pay_fwd))
    mine_b = jnp.stack([*far_bwd, last_bwd])
    other_b = to_core(mine_b)
    near_fwd = near(pay_fwd)
    grads, scale = plain_call(
        backward_kernel,
        (
            jax.ShapeDtypeStruct((tokens + STAT, 3 * local), BF16),
            jax.ShapeDtypeStruct((tokens, HD), F32),
        ),
        "backward",
        6.0,
        ints,
        first,
        first_stat,
        mine_b,
        other_b,
        weight,
        upstream,
        scratch=[
            pltpu.VMEM((tokens, 3 * local), F32),
            proj,
            pltpu.VMEM((tokens, tokens), BF16),
            pltpu.VMEM((tokens, tokens), BF16),
        ],
    )
    near_fwd, grads = tie((near_fwd, grads))
    grads_other = to_core(grads)
    far_fwd = far(near_fwd)
    last_fwd = to_chip(near_fwd[0], FAR[-1])

    def input_grads(places, grads, name, shapes):
        return plain_call(
            functools.partial(input_grad_kernel, places),
            shapes,
            name,
            3.5,
            ints,
            grads,
            grads_other,
            weight,
            w_other,
        )

    for_2, for_5, for_7, for_6 = input_grads((4, 5, 6, 7), grads, "input_grad_far", [block] * 4)
    alone = jax.ShapeDtypeStruct((tokens, local), F32)
    far_fwd, near_fwd, for_2, for_5, for_7, later = tie(
        (far_fwd, near_fwd, for_2, for_5, for_7, grads)
    )
    came = [to_chip(for_7, 3), to_chip(for_5, 4), to_chip(for_2, 1)]
    *parts, own, pair = input_grads(
        (1, 2, 3, 0),
        later,
        "input_grad_near",
        [alone] * 4 + [jax.ShapeDtypeStruct((STAT, local), BF16)],
    )
    last_fwd, pair = tie((last_fwd, pair))
    came[0], for_6 = tie((came[0], for_6))
    direct = to_chip(for_6, 6)
    sums = plain_call(add_kernel, [block] * 3, "add", 1.0, pair, *parts, *came)
    gone = [to_chip(part, d) for part, d in zip(sums, NEAR[1:])] + [direct]
    mine_fa = jnp.stack(near_fwd)
    other_fa = to_core(mine_fa)
    mine_fb = jnp.stack([*far_fwd, last_fwd])
    other_fb = to_core(mine_fb)
    first_f, stat_f = plain_call(
        first_kernel, (wide, stat), "first_fwd", 2.5, ints, mine_fa, other_fa, weight
    )
    result = plain_call(
        forward_kernel,
        narrow,
        "forward",
        4.5,
        ints,
        first_f,
        stat_f,
        mine_fb,
        other_fb,
        weight,
        forward_in,
        scratch=[proj],
    )
    sent_on = shifted(result, "section", 1)
    gone, result = tie((gone, result))
    grad_w = weight_grad(ints, (mine_a, other_a, mine_b, other_b), grads)
    grad_x, grad_gain = plain_call(
        finish_kernel,
        (narrow, jax.ShapeDtypeStruct((1, local), F32)),
        "finish",
        1.0,
        own,
        pair,
        *gone,
        saved_in,
        upstream,
        gain,
        scale,
    )
    sent_back = shifted(grad_x, "section", -1)
    return (sent_on[None], sent_back[None], jnp.transpose(grad_w, (1, 0, 2))[None], grad_gain)


def solution(mesh):
    in_specs = (
        P("section", None, "fsdp"),
        P("section", None, "fsdp"),
        P("section", None, "fsdp"),
        P("section", None, None, "fsdp"),
        P("section", "fsdp"),
        P(),
        P("section", None),
    )
    out_specs = (
        P("section", None, "fsdp"),
        P("section", None, "fsdp"),
        P("section", None, None, "fsdp"),
        P("section", "fsdp"),
    )
    return jax.shard_map(
        on_device, mesh=mesh, in_specs=in_specs, out_specs=out_specs, check_vma=False
    )
```

```python
import functools
import math

import jax
import jax.numpy as jnp
from jax import lax
from jax.experimental import pallas as pl
from jax.experimental.pallas import tpu as pltpu
from jax.sharding import PartitionSpec as P

HD = 128
BLK = 128
EPS = 1e-05
STAT = 16
CHIPS = 8
F32 = jnp.float32
BF16 = jnp.bfloat16
VMEM_BYTES = 16 << 20


def pieces(row):
    high = row.astype(BF16).astype(F32)
    rest = row - high
    mid = rest.astype(BF16).astype(F32)
    return high, mid, rest - mid


def stat_rows(row, width):
    span = row.shape[1]
    index = lax.broadcasted_iota(jnp.int32, (STAT, width), 0)
    out = jnp.zeros((STAT, width), F32)
    for i, part in enumerate(pieces(row)):
        for j, start in enumerate(range(0, span, width)):
            held = part[:, start : start + width]
            if held.shape[1] < width:
                held = jnp.concatenate(
                    [held, jnp.zeros((1, width - held.shape[1]), F32)], axis=1
                )
            out = jnp.where(index == 3 * j + i, jnp.broadcast_to(held, (STAT, width)), out)
    return out.astype(BF16)


def stat_row(rows, span):
    width = rows.shape[1]
    parts = []
    for j, start in enumerate(range(0, span, width)):
        part = rows[3 * j : 3 * j + 1] + rows[3 * j + 1 : 3 * j + 2] + rows[3 * j + 2 : 3 * j + 3]
        parts.append(part[:, : min(width, span - start)])
    return parts[0] if len(parts) == 1 else jnp.concatenate(parts, axis=1)


def as_column(row):
    return jnp.transpose(jnp.broadcast_to(row, (HD, row.shape[1])))


def row_sums(folded):
    return jnp.sum(jnp.transpose(folded), axis=0, keepdims=True)


def pack_kernel(x_hbm, gain_hbm, out_ref, x_ref, gain_ref, sem_ref):
    copies = [
        pltpu.make_async_copy(x_hbm, x_ref, sem_ref.at[0]),
        pltpu.make_async_copy(gain_hbm, gain_ref, sem_ref.at[1]),
    ]
    for held in copies:
        held.start()
    for held in copies:
        held.wait()
    tokens = x_ref.shape[0]
    wide = x_ref[...].astype(F32)
    out_ref[:tokens, :] = (wide * gain_ref[...]).astype(BF16)
    squares = wide * wide
    folded = squares[:, :HD]
    for start in range(HD, squares.shape[1], HD):
        folded = folded + squares[:, start : start + HD]
    out_ref[tokens:, :] = stat_rows(row_sums(folded), out_ref.shape[1])


def listed(ints_ref, which, b, shape, dim):
    z = ints_ref[48 + which]
    block = lax.shift_right_logical(
        lax.broadcasted_iota(jnp.int32, shape, dim), BLK.bit_length() - 1
    )
    return (block == ints_ref[z * 6 + b * 2]) | (block == ints_ref[z * 6 + b * 2 + 1])


def contract(left, right, left_dim, right_dim):
    return lax.dot_general(
        left, right, (((left_dim,), (right_dim,)), ((), ())), preferred_element_type=F32
    )


def softmax(scores, mask, axis):
    scores = jnp.where(mask, scores * (1.0 / math.sqrt(HD)), -1e30)
    expd = jnp.exp(scores - jnp.max(scores, axis=axis, keepdims=True))
    return expd * (1.0 / jnp.sum(expd, axis=axis, keepdims=True))


def partial_product(ints_ref, at, mine_ref, other_ref, w_ref, tokens):
    count, _, local = mine_ref.shape
    both = [(ref, i) for i in range(count) for ref in (mine_ref, other_ref)]
    x_all = jnp.concatenate([ref[i, :tokens, :] for ref, i in both], axis=1)
    places = [ints_ref[50 + side * 8 + at + i] for i in range(count) for side in range(2)]
    parts = []
    for j in range(3):
        w_all = jnp.concatenate(
            [w_ref[j, pl.ds(pl.multiple_of(p * local, local), local), :] for p in places], axis=0
        )
        parts.append(jnp.dot(x_all, w_all, preferred_element_type=F32))
    stats = sum(ref[i, tokens:, :].astype(F32) for ref, i in both)
    return parts, stats


def first_kernel(ints_ref, mine_ref, other_ref, w_ref, acc_ref, stat_ref):
    tokens = acc_ref.shape[0]
    local = mine_ref.shape[2]
    parts, stats = partial_product(ints_ref, 0, mine_ref, other_ref, w_ref, tokens)
    for j, part in enumerate(parts):
        acc_ref[:, j * local : (j + 1) * local] = part
    stat_ref[...] = stats


def finish_product(ints_ref, first_ref, stat_ref, mine_ref, other_ref, w_ref, acc_ref, proj_ref):
    tokens = first_ref.shape[0]
    local = mine_ref.shape[2]
    parts, stats = partial_product(ints_ref, 4, mine_ref, other_ref, w_ref, tokens)
    width = 2 * CHIPS * local
    scale = lax.rsqrt(as_column(stat_row(stat_ref[...] + stats, tokens)) / width + EPS)
    for j, part in enumerate(parts):
        for start in range(0, local, HD):
            cols = slice(j * local + start, j * local + start + HD)
            whole = first_ref[:, cols] + part[:, start : start + HD]
            if acc_ref is not None:
                acc_ref[:, cols] = whole
            proj_ref[:, cols] = (scale * whole).astype(BF16)
    return scale


def forward_kernel(
    ints_ref, first_ref, stat_ref, mine_ref, other_ref, w_ref, x_ref, out_ref, proj_ref
):
    tokens, local = x_ref.shape
    finish_product(ints_ref, first_ref, stat_ref, mine_ref, other_ref, w_ref, None, proj_ref)
    for b in range(tokens // BLK):
        rows = slice(b * BLK, (b + 1) * BLK)
        mask = listed(ints_ref, 0, b, (BLK, tokens), 1)
        for h in range(local // HD):
            at = h * HD
            key_in = proj_ref[:, local + at : local + at + HD]
            value = proj_ref[:, 2 * local + at : 2 * local + at + HD]
            scores = contract(proj_ref[rows, at : at + HD], key_in, 1, 1)
            probs = softmax(scores, mask, 1)
            attn = jnp.dot(probs.astype(BF16), value, preferred_element_type=F32)
            out_ref[rows, at : at + HD] = (x_ref[rows, at : at + HD].astype(F32) + attn).astype(
                BF16
            )


def backward_kernel(
    ints_ref,
    first_ref,
    stat_ref,
    mine_ref,
    other_ref,
    w_ref,
    c_ref,
    out_ref,
    scale_ref,
    acc_ref,
    proj_ref,
    p_ref,
    s_ref,
):
    tokens, local = c_ref.shape
    scale = finish_product(
        ints_ref, first_ref, stat_ref, mine_ref, other_ref, w_ref, acc_ref, proj_ref
    )
    scale_ref[...] = scale
    folded = jnp.zeros((tokens, HD), F32)
    masks = [listed(ints_ref, 1, b, (tokens, BLK), 0) for b in range(tokens // BLK)]
    for h in range(local // HD):
        at = h * HD
        query = proj_ref[:, at : at + HD]
        key_in = proj_ref[:, local + at : local + at + HD]
        value = proj_ref[:, 2 * local + at : 2 * local + at + HD]
        upstream = c_ref[:, at : at + HD]
        for b, mask in enumerate(masks):
            cols = slice(b * BLK, (b + 1) * BLK)
            probs = softmax(contract(key_in, query[cols], 1, 1), mask, 0)
            grad_p = contract(value, upstream[cols], 1, 1)
            inner = jnp.sum(probs * grad_p, axis=0, keepdims=True)
            p_ref[:, cols] = probs.astype(BF16)
            s_ref[:, cols] = (probs * (grad_p - inner) * (1.0 / math.sqrt(HD))).astype(BF16)
        grad_s = s_ref[...]
        parts = (
            contract(grad_s, key_in, 0, 0),
            jnp.dot(grad_s, query, preferred_element_type=F32),
            jnp.dot(p_ref[...], upstream, preferred_element_type=F32),
        )
        for j, part in enumerate(parts):
            cols = slice(j * local + at, j * local + at + HD)
            grads = (scale * part).astype(BF16)
            out_ref[:tokens, cols] = grads
            folded = folded + grads.astype(F32) * acc_ref[:, cols]
    out_ref[tokens:, :] = stat_rows(row_sums(folded), out_ref.shape[1])


def input_grad_kernel(places, ints_ref, mine_ref, other_ref, w_mine_ref, w_other_ref, *out_refs):
    tokens = mine_ref.shape[0] - STAT
    local = w_mine_ref.shape[2]
    grads = jnp.concatenate([mine_ref[:tokens, :], other_ref[:tokens, :]], axis=1)
    totals = stat_row(mine_ref[tokens:, :].astype(F32) + other_ref[tokens:, :].astype(F32), tokens)
    stats = stat_rows(totals, local)
    for place, ref in zip(places, out_refs):
        rows = pl.ds(pl.multiple_of(ints_ref[50 + place] * local, local), local)
        w_all = jnp.concatenate(
            [w[j, rows, :] for w in (w_mine_ref, w_other_ref) for j in range(3)], axis=1
        )
        ref[:tokens, :] = contract(grads, w_all, 1, 1).astype(ref.dtype)
        if ref.shape[0] > tokens:
            ref[tokens:, :] = stats
    if len(out_refs) > len(places):
        out_refs[-1][...] = stats


def add_kernel(pair_ref, *refs):
    count = len(refs) // 3
    pair = pair_ref[...].astype(F32)
    for part, came, out in zip(refs[:count], refs[count : 2 * count], refs[2 * count :]):
        tokens = part.shape[0]
        out[:tokens, :] = (part[...] + came[:tokens, :].astype(F32)).astype(BF16)
        total = stat_row(pair + came[tokens:, :].astype(F32), tokens)
        out[tokens:, :] = stat_rows(total, out.shape[1])


def weight_grad_kernel(
    ints_ref, mine_ref, other_ref, more_ref, rest_ref, g_ref, out_ref, buf_ref, sem_ref
):
    tokens = g_ref.shape[0] - STAT
    half, _, local = mine_ref.shape
    side = ints_ref[66]
    grads = g_ref[:tokens, :]

    def copy(piece, j, row):
        return pltpu.make_async_copy(
            buf_ref.at[piece, j], out_ref.at[j, pl.ds(row, local), :], sem_ref.at[piece, j]
        )

    copies = []
    for s, pair in enumerate(((mine_ref, other_ref), (more_ref, rest_ref))):
        for i in range(half):
            for k, ref in enumerate(pair):
                piece = (s * half + i) * 2 + k
                place = ints_ref[67 + s * half + i] * 2 + (side if k == 0 else 1 - side)
                part = contract(ref[i, :tokens, :], grads, 0, 0)
                for j in range(3):
                    buf_ref[piece, j] = part[:, j * local : (j + 1) * local].astype(BF16)
                    copies.append(copy(piece, j, pl.multiple_of(place * local, local)))
                    copies[-1].start()
    for held in copies:
        held.wait()


def weight_grad(ints, blocks, grads):
    chips, rows, local = 2 * blocks[0].shape[0], *blocks[0].shape[1:]
    vmem = pl.BlockSpec(memory_space=pltpu.VMEM)
    return pl.pallas_call(
        weight_grad_kernel,
        out_shape=jax.ShapeDtypeStruct((3, 2 * chips * local, local), BF16),
        in_specs=[pl.BlockSpec(memory_space=pltpu.SMEM), *([vmem] * 5)],
        out_specs=pl.BlockSpec(memory_space=pltpu.HBM),
        scratch_shapes=[
            pltpu.VMEM((2 * chips, 3, local, local), BF16),
            pltpu.SemaphoreType.DMA((2 * chips, 3)),
        ],
        compiler_params=pltpu.CompilerParams(vmem_limit_bytes=VMEM_BYTES),
        cost_estimate=cost(5.0),
        name="weight_grad",
    )(ints, *blocks, grads)


def finish_kernel(own_ref, pair_ref, *refs):
    blocks, (x_ref, c_ref, gain_ref, scale_ref, dx_ref, gg_ref) = refs[:-6], refs[-6:]
    tokens, local = x_ref.shape
    own_in = own_ref[...]
    stats = pair_ref[...].astype(F32)
    for ref in blocks:
        own_in = own_in + ref[:tokens, :].astype(F32)
        stats = stats + ref[tokens:, :].astype(F32)
    total = as_column(stat_row(stats, tokens))
    scale = scale_ref[...]
    factor = scale * scale * total / (2 * CHIPS * local)
    x_wide = x_ref[...].astype(F32)
    for start in range(0, local, HD):
        cols = slice(start, start + HD)
        grad_x = c_ref[:, cols].astype(F32) + gain_ref[:, cols] * own_in[:, cols]
        dx_ref[:, cols] = (grad_x - factor * x_wide[:, cols]).astype(BF16)
    gg_ref[...] = jnp.sum(x_wide * own_in, axis=0, keepdims=True)


def cost(us):
    return pl.CostEstimate(flops=int(us * 1.1e9), transcendentals=0, bytes_accessed=0)


def plain_call(kernel, out_shape, name, us, *args, scratch=(), held=True):
    vmem = pl.BlockSpec(memory_space=pltpu.VMEM) if held else pl.BlockSpec()
    specs = [
        pl.BlockSpec(memory_space=pltpu.SMEM) if a.dtype == jnp.int32 else vmem for a in args
    ]
    return pl.pallas_call(
        kernel,
        out_shape=out_shape,
        in_specs=specs,
        out_specs=jax.tree.map(lambda s: vmem, out_shape),
        scratch_shapes=list(scratch),
        compiler_params=pltpu.CompilerParams(vmem_limit_bytes=VMEM_BYTES),
        cost_estimate=cost(us),
        name=name,
    )(*args)


def pack(x, gain, name):
    tokens, local = x.shape
    hbm = pl.BlockSpec(memory_space=pltpu.HBM)
    return pl.pallas_call(
        pack_kernel,
        out_shape=jax.ShapeDtypeStruct((tokens + STAT, local), BF16),
        in_specs=[hbm, hbm],
        out_specs=pl.BlockSpec(memory_space=pltpu.VMEM),
        scratch_shapes=[
            pltpu.VMEM((tokens, local), BF16),
            pltpu.VMEM((1, local), F32),
            pltpu.SemaphoreType.DMA((2,)),
        ],
        compiler_params=pltpu.CompilerParams(vmem_limit_bytes=VMEM_BYTES),
        cost_estimate=cost(1.0),
        name=name,
    )(x, gain)


def to_chip(block, distance):
    route = [(i, ((i >> 1) ^ distance) << 1 | (i & 1)) for i in range(2 * CHIPS)]
    return lax.ppermute(block, "fsdp", route)


def to_core(block):
    return lax.ppermute(block, "fsdp", [(i, i ^ 1) for i in range(2 * CHIPS)])


def shifted(block, axis, distance):
    count = lax.axis_size(axis)
    return lax.ppermute(block, axis, [((i - distance) % count, i) for i in range(count)])


NEAR = (0, 4, 1, 3)
FAR = (2, 5, 7, 6)
tie = lax.optimization_barrier


def near(block):
    return [block] + [to_chip(block, d) for d in NEAR[1:]]


def far(blocks):
    _, by_x, by_1, by_3 = blocks
    return [to_chip(by_3, 1), to_chip(by_1, 4), to_chip(by_x, 3)]


def on_device(x_fwd, x_saved, cotangent, qkv_weight, gain, block_lists, plan):
    forward_in = x_fwd[0]
    saved_in = x_saved[0]
    upstream = cotangent[0]
    weight = jnp.transpose(qkv_weight[0], (1, 0, 2))
    tokens, local = forward_in.shape
    me = lax.axis_index("fsdp").astype(jnp.int32)
    chip, side = me // 2, me % 2
    apart = jnp.array(NEAR + FAR, dtype=jnp.int32) ^ chip
    ints = jnp.concatenate(
        [
            block_lists.reshape(-1),
            plan.reshape(-1),
            apart * 2 + side,
            apart * 2 + 1 - side,
            side[None],
            apart,
        ]
    )
    block = jax.ShapeDtypeStruct((tokens + STAT, local), BF16)
    wide = jax.ShapeDtypeStruct((tokens, 3 * local), F32)
    stat = jax.ShapeDtypeStruct((STAT, local), F32)
    narrow = jax.ShapeDtypeStruct((tokens, local), BF16)
    proj = pltpu.VMEM((tokens, 3 * local), BF16)

    pay_bwd = pack(saved_in, gain, "pack_bwd")
    pay_fwd = pack(forward_in, gain, "pack_fwd")
    w_other = to_core(weight)

    near_bwd = near(pay_bwd)
    pay_bwd, pay_fwd = tie((pay_bwd, pay_fwd))
    last_bwd = to_chip(pay_bwd, FAR[-1])
    near_bwd, pay_fwd = tie((near_bwd, pay_fwd))
    mine_a = jnp.stack(near_bwd)
    other_a = to_core(mine_a)
    far_bwd = far(near_bwd)
    first, first_stat = plain_call(
        first_kernel, (wide, stat), "first_bwd", 2.5, ints, mine_a, other_a, weight
    )
    last_bwd, first, w_other, pay_fwd = tie((last_bwd, first, w_other, pay_fwd))
    mine_b = jnp.stack([*far_bwd, last_bwd])
    other_b = to_core(mine_b)
    near_fwd = near(pay_fwd)
    grads, scale = plain_call(
        backward_kernel,
        (
            jax.ShapeDtypeStruct((tokens + STAT, 3 * local), BF16),
            jax.ShapeDtypeStruct((tokens, HD), F32),
        ),
        "backward",
        6.0,
        ints,
        first,
        first_stat,
        mine_b,
        other_b,
        weight,
        upstream,
        scratch=[
            pltpu.VMEM((tokens, 3 * local), F32),
            proj,
            pltpu.VMEM((tokens, tokens), BF16),
            pltpu.VMEM((tokens, tokens), BF16),
        ],
    )
    near_fwd, grads = tie((near_fwd, grads))
    grads_other = to_core(grads)
    far_fwd = far(near_fwd)
    last_fwd = to_chip(near_fwd[0], FAR[-1])

    def input_grads(places, grads, name, shapes):
        return plain_call(
            functools.partial(input_grad_kernel, places),
            shapes,
            name,
            3.5,
            ints,
            grads,
            grads_other,
            weight,
            w_other,
        )

    for_2, for_5, for_7, for_6 = input_grads((4, 5, 6, 7), grads, "input_grad_far", [block] * 4)
    alone = jax.ShapeDtypeStruct((tokens, local), F32)
    later, for_7 = tie((grads, for_7))
    came = [to_chip(for_7, 3), to_chip(for_5, 4), to_chip(for_2, 1)]
    *parts, own, pair = input_grads(
        (1, 2, 3, 0),
        later,
        "input_grad_near",
        [alone] * 4 + [jax.ShapeDtypeStruct((STAT, local), BF16)],
    )
    far_fwd, near_fwd, last_fwd, pair = tie((far_fwd, near_fwd, last_fwd, pair))
    grad_w = weight_grad(ints, (mine_a, other_a, mine_b, other_b), grads)
    came, for_6, grad_w = tie((came, for_6, grad_w))
    direct = to_chip(for_6, 6)
    sums = plain_call(add_kernel, [block] * 3, "add", 1.0, pair, *parts, *came)
    gone = [to_chip(part, d) for part, d in zip(sums, NEAR[1:])] + [direct]
    mine_fa = jnp.stack(near_fwd)
    other_fa = to_core(mine_fa)
    mine_fb = jnp.stack([*far_fwd, last_fwd])
    other_fb = to_core(mine_fb)
    first_f, stat_f = plain_call(
        first_kernel, (wide, stat), "first_fwd", 2.5, ints, mine_fa, other_fa, weight
    )
    result = plain_call(
        forward_kernel,
        narrow,
        "forward",
        4.5,
        ints,
        first_f,
        stat_f,
        mine_fb,
        other_fb,
        weight,
        forward_in,
        scratch=[proj],
    )
    sent_on = shifted(result, "section", 1)
    gone, result = tie((gone, result))
    grad_x, grad_gain = plain_call(
        finish_kernel,
        (narrow, jax.ShapeDtypeStruct((1, local), F32)),
        "finish",
        1.0,
        own,
        pair,
        *gone,
        saved_in,
        upstream,
        gain,
        scale,
    )
    sent_back = shifted(grad_x, "section", -1)
    return (sent_on[None], sent_back[None], jnp.transpose(grad_w, (1, 0, 2))[None], grad_gain)


def solution(mesh):
    in_specs = (
        P("section", None, "fsdp"),
        P("section", None, "fsdp"),
        P("section", None, "fsdp"),
        P("section", None, None, "fsdp"),
        P("section", "fsdp"),
        P(),
        P("section", None),
    )
    out_specs = (
        P("section", None, "fsdp"),
        P("section", None, "fsdp"),
        P("section", None, None, "fsdp"),
        P("section", "fsdp"),
    )
    return jax.shard_map(
        on_device, mesh=mesh, in_specs=in_specs, out_specs=out_specs, check_vma=False
    )
```
